32 devices in a mesh: dp: 8 (over z, y), tensor: 4 (over x, core).
Axes of the slice: x: 2, y: 2, z: 4, core: 2. Of those that a mesh axis runs over, the one named last changes fastest.
Arguments:
- block_in: float32 [4096, 640], P(('dp', 'tensor')), may hold values from -6 to 6
- d_output: float32 [4096, 640], P(('dp', 'tensor')), may hold values from -6 to 6
- doc_ids: int32 [8, 512], P('dp'), may hold values from 0 to 3, never falling along the last dimension, each value on 1 to 256 neighbouring positions
- w_query: float32 [640, 1024], P('dp', 'tensor'), may hold values from -0.25 to 0.25
- w_key: float32 [640, 256], P('dp'), may hold values from -0.25 to 0.25
- w_value: float32 [640, 256], P('dp'), may hold values from -0.25 to 0.25
- w_output: float32 [640, 1024], P('dp', 'tensor'), may hold values from -0.1875 to 0.1875
- w_gate: float32 [640, 2048], P('dp', 'tensor'), may hold values from -0.25 to 0.25
- w_up: float32 [640, 2048], P('dp', 'tensor'), may hold values from -0.25 to 0.25
- w_down: float32 [640, 2048], P('dp', 'tensor'), may hold values from -0.125 to 0.125
- mom_query: float32 [640, 1024], P('dp', 'tensor'), may hold values from -112 to 112
- mom_key: float32 [640, 256], P('dp'), may hold values from -112 to 112
- mom_value: float32 [640, 256], P('dp'), may hold values from -112 to 112
- mom_output: float32 [640, 1024], P('dp', 'tensor'), may hold values from -112 to 112
- mom_gate: float32 [640, 2048], P('dp', 'tensor'), may hold values from -112 to 112
- mom_up: float32 [640, 2048], P('dp', 'tensor'), may hold values from -112 to 112
- mom_down: float32 [640, 2048], P('dp', 'tensor'), may hold values from -112 to 112
- gains: float32 [3072], replicated, may hold values from -0.4 to 0.6
- adam_first: float32 [3072], replicated, may hold values from -112 to 112
- adam_second: float32 [3072], replicated, may hold values from 204.8 to 8192
Outputs:
- block_out: float32 [4096, 640], P(('dp', 'tensor'))
- d_input: float32 [4096, 640], P(('dp', 'tensor'))
- grad_query: float32 [640, 1024], P('dp', 'tensor')
- grad_key: float32 [640, 256], P('dp')
- grad_value: float32 [640, 256], P('dp')
- grad_output: float32 [640, 1024], P('dp', 'tensor')
- grad_gate: float32 [640, 2048], P('dp', 'tensor')
- grad_up: float32 [640, 2048], P('dp', 'tensor')
- grad_down: float32 [640, 2048], P('dp', 'tensor')
- grad_gains: float32 [3072], replicated
- new_query: float32 [640, 1024], P('dp', 'tensor')
- new_key: float32 [640, 256], P('dp')
- new_value: float32 [640, 256], P('dp')
- new_output: float32 [640, 1024], P('dp', 'tensor')
- new_gate: float32 [640, 2048], P('dp', 'tensor')
- new_up: float32 [640, 2048], P('dp', 'tensor')
- new_down: float32 [640, 2048], P('dp', 'tensor')
- momentum_query: float32 [640, 1024], P('dp', 'tensor')
- momentum_key: float32 [640, 256], P('dp')
- momentum_value: float32 [640, 256], P('dp')
- momentum_output: float32 [640, 1024], P('dp', 'tensor')
- momentum_gate: float32 [640, 2048], P('dp', 'tensor')
- momentum_up: float32 [640, 2048], P('dp', 'tensor')
- momentum_down: float32 [640, 2048], P('dp', 'tensor')
- new_gains: float32 [3072], replicated
- next_first: float32 [3072], replicated
- next_second: float32 [3072], replicated
The draws below stay inside these ranges and needn't reach their ends.
Inputs may be any that keep to these rules, and one draw needn't show every extreme that they name: `doc_ids`: along each sequence the document id never falls; each document covers 1 to half of 512 tokens, and some document covers exactly half of 512.
All inputs are finite; a program needn't handle non-finite values.
Results may differ from the reference program's by a relative error of at most 0.02.
Values may be sent and summed in bfloat16 or wider, within the bound.
No kernel may reach another device: no remote copies, remote signals or barrier semaphores. Data moves between devices by JAX's collectives and lax.ppermute only.
A program may use at most 64 MiB of HBM per device.

```python
import math
import jax
import jax.numpy as jnp
import numpy as np
from jax import lax

D = 640
H = 4
HD = 256
FF = 2048
SEQ = 512
DOCS = 4
NS_STEPS = 5
STEP = 5
SEQS = 8
TOKENS = 4096


def steps_of(key, extent, shards, low, top_value):
    def one(position, blocks):
        draws = jax.random.uniform(jax.random.fold_in(jax.random.fold_in(key, 6), position), (blocks,), jnp.float32, low / len(shards), top_value / len(shards))
        return jnp.repeat(jnp.exp(draws), extent[position] // blocks).reshape((-1,) + (1,) * (len(extent) - position - 1))

    factor_of = one(*shards[0])
    for cut in shards[1:]:
        factor_of = factor_of * one(*cut)
    return factor_of


def profile(count, total, limit, skew):
    portions = [(1 << 20) // math.isqrt(rank ** skew) + 1 for rank in range(2, count + 1)]
    rest, holding = total - limit - (count - 1), [1] * (count - 1)
    while rest > 0:
        candidates = [i for i in range(count - 1) if holding[i] < limit]
        mass, remaining = sum([portions[i] for i in candidates]), rest
        for i in candidates:
            more = min(limit - holding[i], max(1, remaining * portions[i] // mass), rest)
            holding[i] = holding[i] + more
            rest = rest - more
    return np.array([limit] + holding)


def uneven(own_key, count, total, most, skew):
    if count == 2:
        one = jax.random.randint(own_key, (), max(1, total - most), min(most, total - 1) + 1)
        return jnp.stack([one, total - one])
    lengths = jnp.asarray(profile(count, total, most, skew), jnp.int32)
    pairs = (count - 1) // 2
    donor, receiver = lengths[1:1 + 2 * pairs:2], lengths[2:2 + 2 * pairs:2]
    slack = jnp.minimum(donor - 1, most - receiver)
    shifted = jax.random.randint(jax.random.fold_in(own_key, 1), (pairs,), 0, 1 << 20) % (slack + 1)
    lengths = lengths.at[1:1 + 2 * pairs:2].set(donor - shifted).at[2:2 + 2 * pairs:2].set(receiver + shifted)
    return lengths[jax.random.permutation(jax.random.fold_in(own_key, 2), count)]


def normal_values(own_key, dims, width, most, shards=(), held_as=jnp.bfloat16):
    array = width * jax.random.normal(own_key, dims, jnp.float32)
    if shards:
        array = array * steps_of(own_key, dims, shards, -0.22, 0.18)
    return jnp.clip(array, -most, most).astype(held_as)


def setup_inputs(seed: int = 0) -> dict:
    key_list = jax.random.split(jax.random.key(seed), 21)
    return {
        "block_in": normal_values(key_list[0], (TOKENS, D), 1.0, 6.0, ((0, 32),), jnp.float32),
        "d_output": normal_values(key_list[1], (TOKENS, D), 1.0, 6.0, ((0, 32),), jnp.float32),
        "doc_ids": jax.vmap(lambda own: jnp.searchsorted(jnp.cumsum(uneven(own, DOCS, SEQ, SEQ // 2, 1)), jnp.arange(SEQ), side="right"))(jax.random.split(key_list[2], SEQS)).reshape((SEQS, SEQ)).astype(jnp.int32),
        "w_query": normal_values(key_list[3], (D, H * HD), D ** -0.5, 0.25, ((0, 8), (1, 4)), jnp.float32),
        "w_key": normal_values(key_list[4], (D, HD), D ** -0.5, 0.25, ((0, 8),), jnp.float32),
        "w_value": normal_values(key_list[5], (D, HD), D ** -0.5, 0.25, ((0, 8),), jnp.float32),
        "w_output": normal_values(key_list[6], (D, H * HD), (H * HD) ** -0.5, 0.1875, ((0, 8), (1, 4)), jnp.float32),
        "w_gate": normal_values(key_list[7], (D, FF), D ** -0.5, 0.25, ((0, 8), (1, 4)), jnp.float32),
        "w_up": normal_values(key_list[8], (D, FF), D ** -0.5, 0.25, ((0, 8), (1, 4)), jnp.float32),
        "w_down": normal_values(key_list[9], (D, FF), FF ** -0.5, 0.125, ((0, 8), (1, 4)), jnp.float32),
        "mom_query": normal_values(key_list[10], (D, H * HD), (0.3 * TOKENS ** 0.5), 112.0, ((0, 8), (1, 4)), jnp.float32),
        "mom_key": normal_values(key_list[11], (D, HD), (0.3 * TOKENS ** 0.5), 112.0, ((0, 8),), jnp.float32),
        "mom_value": normal_values(key_list[12], (D, HD), (0.3 * TOKENS ** 0.5), 112.0, ((0, 8),), jnp.float32),
        "mom_output": normal_values(key_list[13], (D, H * HD), (0.3 * TOKENS ** 0.5), 112.0, ((0, 8), (1, 4)), jnp.float32),
        "mom_gate": normal_values(key_list[14], (D, FF), (0.3 * TOKENS ** 0.5), 112.0, ((0, 8), (1, 4)), jnp.float32),
        "mom_up": normal_values(key_list[15], (D, FF), (0.3 * TOKENS ** 0.5), 112.0, ((0, 8), (1, 4)), jnp.float32),
        "mom_down": normal_values(key_list[16], (D, FF), (0.3 * TOKENS ** 0.5), 112.0, ((0, 8), (1, 4)), jnp.float32),
        "gains": jnp.clip(jax.random.uniform(key_list[17], (4 * D + 2 * HD,), jnp.float32, -0.4, 0.6), -0.4, 0.6),
        "adam_first": normal_values(key_list[18], (4 * D + 2 * HD,), (0.3 * TOKENS ** 0.5), 112.0, (), jnp.float32),
        "adam_second": jnp.clip(jnp.exp(jax.random.uniform(key_list[19], (4 * D + 2 * HD,), jnp.float32, math.log(204.8), math.log(8192.0))), 204.8, 8192.0),
    }


EPSILON = 1e-06
ROPE_BASE = 10000.0
MUON_BETA = 0.95
MUON_RATE = 0.04
MUON_DECAY = 0.1
POLY_FIRST = 3.4445
POLY_SECOND = -4.775
POLY_THIRD = 2.0315
FIRST_DECAY = 0.9
SECOND_DECAY = 0.95
ADAM_RATE = 0.05
ADAM_EPSILON = 1e-08
MASKED = -1e+30

def rms_norm(values, gain):
    factor = lax.rsqrt(lax.optimization_barrier(jnp.mean(values * values, axis=-1, keepdims=True)) + EPSILON)
    return values * factor * (1.0 + gain)

def rotate(values, cosine, sine):
    half = values.shape[-1] // 2
    turned = jnp.concatenate([-values[..., half:], values[..., :half]], axis=-1)
    return values * cosine + turned * sine

def head_map(raw, gain, cosine, sine):
    return rotate(rms_norm(raw, gain), cosine, sine)

def gated(gate, upper):
    return jax.nn.gelu(gate, approximate=True) * upper

def rope_tables(doc_rows, head_width):
    length = doc_rows.shape[-1]
    first = lax.optimization_barrier(jnp.sum((doc_rows[..., None, :] < doc_rows[..., :, None]).astype(jnp.int32), axis=-1))
    offset = (jnp.arange(length, dtype=jnp.int32) - first).astype(jnp.float32)
    freqs = ROPE_BASE ** (-(2.0 * jnp.arange(head_width // 2, dtype=jnp.float32)) / head_width)
    angles = offset[..., None] * freqs
    angles = jnp.concatenate([angles, angles], axis=-1)
    return (jnp.cos(angles), jnp.sin(angles))

def forward_backward(rows_in, cotangent, doc_row, low, gains):
    wq16, wk16, wv16, wo16, wg16, wu16, wd16 = low
    pre_attn = gains[0:D]
    post_attn = gains[D:2 * D]
    pre_ffn = gains[2 * D:3 * D]
    post_ffn = gains[3 * D:4 * D]
    gain_q = gains[4 * D:4 * D + HD]
    gain_k = gains[4 * D + HD:]
    f32 = jnp.float32
    bf16 = jnp.bfloat16
    cosine, sine = rope_tables(doc_row, HD)
    places = jnp.arange(SEQ)
    allowed = (doc_row[None, :] == doc_row[:, None]) & (places[None, :] <= places[:, None])
    scale = HD ** (-0.5)
    normed_one = rms_norm(rows_in, pre_attn).astype(bf16)
    queries = jnp.dot(normed_one, wq16, preferred_element_type=f32).reshape(SEQ, H, HD)
    keys = jnp.dot(normed_one, wk16, preferred_element_type=f32)
    values = jnp.dot(normed_one, wv16, preferred_element_type=f32).astype(bf16)
    query_rot = head_map(queries, gain_q, cosine[:, None, :], sine[:, None, :]).astype(bf16)
    key_rot = head_map(keys, gain_k, cosine, sine).astype(bf16)
    scores = jnp.einsum('shd,td->hst', query_rot.astype(f32), key_rot.astype(f32)) * scale
    scores = jnp.where(allowed[None], scores, MASKED)
    top = lax.optimization_barrier(jnp.max(scores, axis=-1, keepdims=True))
    log_total = top + jnp.log(lax.optimization_barrier(jnp.sum(jnp.exp(scores - top), axis=-1, keepdims=True)))
    probs = jnp.exp(scores - log_total).astype(bf16)
    heads = jnp.einsum('hst,td->shd', probs.astype(f32), values.astype(f32)).astype(bf16)
    heads_flat = heads.reshape(SEQ, H * HD)
    attn = jnp.dot(heads_flat, wo16.T, preferred_element_type=f32)
    middle = rows_in + rms_norm(attn, post_attn)
    normed_two = rms_norm(middle, pre_ffn).astype(bf16)
    gate = jnp.dot(normed_two, wg16, preferred_element_type=f32)
    upper = jnp.dot(normed_two, wu16, preferred_element_type=f32)
    hidden = gated(gate, upper).astype(bf16)
    branch = jnp.dot(hidden, wd16.T, preferred_element_type=f32)
    output = middle + rms_norm(branch, post_ffn)
    pull = jax.vjp(rms_norm, branch, post_ffn)[1]
    d_branch, g_post_ffn = pull(cotangent)
    branch_low = d_branch.astype(bf16)
    grad_down = jnp.dot(branch_low.T, hidden, preferred_element_type=f32)
    d_hidden = jnp.dot(branch_low, wd16, preferred_element_type=f32)
    pull = jax.vjp(gated, gate, upper)[1]
    d_gate, d_upper = pull(d_hidden)
    gate_low = d_gate.astype(bf16)
    upper_low = d_upper.astype(bf16)
    grad_gate = jnp.dot(normed_two.T, gate_low, preferred_element_type=f32)
    grad_up = jnp.dot(normed_two.T, upper_low, preferred_element_type=f32)
    d_normed_two = jnp.dot(gate_low, wg16.T, preferred_element_type=f32) + jnp.dot(upper_low, wu16.T, preferred_element_type=f32)
    pull = jax.vjp(rms_norm, middle, pre_ffn)[1]
    d_mid_extra, g_pre_ffn = pull(d_normed_two)
    d_middle = cotangent + d_mid_extra
    pull = jax.vjp(rms_norm, attn, post_attn)[1]
    d_attn, g_post_attn = pull(d_middle)
    attn_low = d_attn.astype(bf16)
    grad_output = jnp.dot(attn_low.T, heads_flat, preferred_element_type=f32)
    d_heads = jnp.dot(attn_low, wo16, preferred_element_type=f32).astype(bf16).reshape(SEQ, H, HD)
    again = jnp.einsum('shd,td->hst', query_rot.astype(f32), key_rot.astype(f32)) * scale
    again = jnp.where(allowed[None], again, MASKED)
    prob_full = jnp.exp(again - log_total)
    delta = jnp.einsum('shd,shd->hs', d_heads.astype(f32), heads.astype(f32))
    d_probs = jnp.einsum('shd,td->hst', d_heads.astype(f32), values.astype(f32))
    d_scores = (prob_full * (d_probs - delta[..., None]) * scale).astype(bf16)
    d_qrot = jnp.einsum('hst,td->shd', d_scores.astype(f32), key_rot.astype(f32))
    d_krot = jnp.einsum('hst,shd->htd', d_scores.astype(f32), query_rot.astype(f32))
    d_vals = jnp.einsum('hst,shd->htd', probs.astype(f32), d_heads.astype(f32))
    pull = jax.vjp(lambda raw, gain: head_map(raw, gain, cosine[:, None, :], sine[:, None, :]), queries, gain_q)[1]
    d_queries, g_query = pull(d_qrot)
    pull = jax.vjp(lambda raw, gain: head_map(raw, gain, cosine, sine), keys, gain_k)[1]
    d_keys, g_key_heads = jax.vmap(pull)(d_krot)
    g_key = lax.optimization_barrier(jnp.sum(g_key_heads, axis=0))
    query_low = d_queries.reshape(SEQ, H * HD).astype(bf16)
    key_low = d_keys.astype(bf16)
    value_low = d_vals.astype(bf16)
    grad_query = jnp.dot(normed_one.T, query_low, preferred_element_type=f32)
    grad_key = jnp.einsum('sd,hse->de', normed_one.astype(f32), key_low.astype(f32))
    grad_value = jnp.einsum('sd,hse->de', normed_one.astype(f32), value_low.astype(f32))
    d_normed_one = jnp.dot(query_low, wq16.T, preferred_element_type=f32)
    d_normed_one = d_normed_one + jnp.einsum('hse,de->sd', key_low.astype(f32), wk16.astype(f32))
    d_normed_one = d_normed_one + jnp.einsum('hse,de->sd', value_low.astype(f32), wv16.astype(f32))
    pull = jax.vjp(rms_norm, rows_in, pre_attn)[1]
    d_in_extra, g_pre_attn = pull(d_normed_one)
    d_rows = d_middle + d_in_extra
    gain_grad = jnp.concatenate([g_pre_attn, g_post_attn, g_pre_ffn, g_post_ffn, g_query, g_key])
    grads = (grad_query, grad_key, grad_value, grad_output, grad_gate, grad_up, grad_down, gain_grad)
    return (output, d_rows, grads)

def muon(weight, moment, grad):
    f32 = jnp.float32
    bf16 = jnp.bfloat16
    moment_new = MUON_BETA * moment + grad
    push = (grad + MUON_BETA * moment_new).astype(bf16)
    push_wide = push.astype(f32)
    ortho = (push_wide / (jnp.sqrt(jnp.sum(push_wide * push_wide)) + 1e-07)).astype(bf16)
    for index in range(NS_STEPS):
        square = jnp.dot(ortho, ortho.T, preferred_element_type=f32).astype(bf16)
        once = jnp.dot(square, ortho, preferred_element_type=f32).astype(bf16)
        twice = jnp.dot(square, once, preferred_element_type=f32)
        ortho = (POLY_FIRST * ortho.astype(f32) + POLY_SECOND * once.astype(f32) + POLY_THIRD * twice).astype(bf16)
    factor = 0.2 * math.sqrt(max(weight.shape[0], weight.shape[1]))
    new_weight = weight - MUON_RATE * (factor * ortho.astype(f32) + MUON_DECAY * weight)
    return (new_weight, moment_new)

def reference(block_in, d_output, doc_ids, w_query, w_key, w_value, w_output, w_gate, w_up, w_down, mom_query, mom_key, mom_value, mom_output, mom_gate, mom_up, mom_down, gains, adam_first, adam_second):
    weights = (w_query, w_key, w_value, w_output, w_gate, w_up, w_down)
    moments = (mom_query, mom_key, mom_value, mom_output, mom_gate, mom_up, mom_down)
    low = tuple((weight.astype(jnp.bfloat16) for weight in weights))
    rows = block_in.reshape(SEQS, SEQ, D)
    cots = d_output.reshape(SEQS, SEQ, D)

    def step_fn(carry, packed):
        seq_in, seq_cot, seq_doc = packed
        output, d_rows, grads = forward_backward(seq_in, seq_cot, seq_doc, low, gains)
        carry = tuple((total + extra for total, extra in zip(carry, grads)))
        return (carry, (output, d_rows))
    zeros = tuple((jnp.zeros(weight.shape, jnp.float32) for weight in weights)) + (jnp.zeros(gains.shape, jnp.float32),)
    totals, stacked = lax.scan(step_fn, zeros, (rows, cots, doc_ids))
    block_out = stacked[0].reshape(TOKENS, D)
    d_input = stacked[1].reshape(TOKENS, D)
    results = [muon(weights[index], moments[index], totals[index]) for index in range(7)]
    grad_gains = totals[7]
    next_first = FIRST_DECAY * adam_first + (1.0 - FIRST_DECAY) * grad_gains
    next_second = SECOND_DECAY * adam_second + (1.0 - SECOND_DECAY) * grad_gains * grad_gains
    first_fix = 1.0 - FIRST_DECAY ** STEP
    second_fix = 1.0 - SECOND_DECAY ** STEP
    new_gains = gains - ADAM_RATE * (next_first / first_fix) / (jnp.sqrt(next_second / second_fix) + ADAM_EPSILON)
    return (block_out, d_input, totals[0], totals[1], totals[2], totals[3], totals[4], totals[5], totals[6], grad_gains, results[0][0], results[1][0], results[2][0], results[3][0], results[4][0], results[5][0], results[6][0], results[0][1], results[1][1], results[2][1], results[3][1], results[4][1], results[5][1], results[6][1], new_gains, next_first, next_second)
```

```python
import math

import jax
import jax.numpy as jnp
from jax import lax
from jax.sharding import PartitionSpec as P

NS_STEPS = 5
STEP = 5


EPSILON = 1e-06
ROPE_BASE = 10000.0
MUON_BETA = 0.95
MUON_RATE = 0.04
MUON_DECAY = 0.1
POLY_FIRST = 3.4445
POLY_SECOND = -4.775
POLY_THIRD = 2.0315
FIRST_DECAY = 0.9
SECOND_DECAY = 0.95
ADAM_RATE = 0.05
ADAM_EPSILON = 1e-08
MASKED = -1e30


def rms_factor(values):
    return lax.rsqrt(jnp.mean(values * values, axis=-1, keepdims=True) + EPSILON)


def rms_norm(values, gain):
    return values * rms_factor(values) * (1.0 + gain)


def rms_pull(values, gain, cotangent):
    factor = rms_factor(values)
    scaled = cotangent * (1.0 + gain)
    inner = jnp.mean(values * scaled, axis=-1, keepdims=True)
    d_values = factor * scaled - values * (factor * factor * factor * inner)
    return d_values, cotangent * values * factor


def rotate(values, cosine, sine):
    half = values.shape[-1] // 2
    turned = jnp.concatenate([-values[..., half:], values[..., :half]], axis=-1)
    return values * cosine + turned * sine


def rotate_back(values, cosine, sine):
    half = values.shape[-1] // 2
    turned = values * sine
    turned = jnp.concatenate([turned[..., half:], -turned[..., :half]], axis=-1)
    return values * cosine + turned


def gated(gate, upper):
    return jax.nn.gelu(gate, approximate=True) * upper


def swap(values, axis, mask):
    count = lax.axis_size(axis)
    return lax.ppermute(values, axis, [(i, i ^ mask) for i in range(count)])


def few(count):
    return 2 <= count <= 8 and count & (count - 1) == 0


def dot(left, right):
    return jnp.dot(left, right, preferred_element_type=jnp.float32)


def dot_rows(left, right):
    return lax.dot_general(
        left, right, (((0,), (0,)), ((), ())), preferred_element_type=jnp.float32
    )


def dot_cols(left, right):
    return lax.dot_general(
        left, right, (((1,), (1,)), ((), ())), preferred_element_type=jnp.float32
    )


def gather_data(block):
    count = lax.axis_size("dp")
    if not few(count):
        return lax.all_gather(block, "dp", axis=0, tiled=True)
    me = lax.axis_index("dp")
    mine = jnp.stack([block] + [swap(block, "dp", 2 * j) for j in range(1, count // 2)])
    other = swap(mine, "dp", 1)
    both = (mine, other)
    parts = []
    for n in range(count):
        parts.append(
            jnp.where(
                (me & 1) == (n & 1),
                lax.dynamic_index_in_dim(mine, (me ^ n) >> 1, 0, keepdims=False),
                lax.dynamic_index_in_dim(other, (me ^ n) >> 1, 0, keepdims=False),
            )
        )
    return jnp.concatenate(parts, axis=0)


def scatter_data(part):
    bf16 = jnp.bfloat16
    count = lax.axis_size("dp")
    if not few(count):
        return lax.psum_scatter(part, "dp", scatter_dimension=0, tiled=True)
    me = lax.axis_index("dp")
    low, high = me & 1, me >> 1
    rows = part.shape[0] // count
    blocks = part.reshape(count // 2, 2, rows, part.shape[1])
    away = lax.dynamic_index_in_dim(blocks, 1 - low, 1, keepdims=False).astype(bf16)
    here = lax.dynamic_index_in_dim(blocks, low, 1, keepdims=False)
    pair = here + swap(away, "dp", 1).astype(jnp.float32)
    narrow = pair.astype(bf16)
    total = lax.dynamic_index_in_dim(pair, high, 0, keepdims=False)
    for j in range(1, count // 2):
        sent = lax.dynamic_index_in_dim(narrow, high ^ j, 0, keepdims=False)
        total = total + swap(sent, "dp", 2 * j).astype(jnp.float32)
    return total


def half_sum(part):
    half = part.shape[0] // 2
    got = swap(part[half:].astype(jnp.bfloat16), "tensor", 1)
    return (part[:half] + got.astype(jnp.float32)).astype(jnp.bfloat16)


def row_sum(part):
    kept = half_sum(part)
    got = swap(kept, "tensor", 2)
    block = kept.shape[0] // 2
    got = jnp.concatenate([got[block:], got[:block]], axis=0)
    return kept.astype(jnp.float32) + got.astype(jnp.float32)


def row_sum_own(part):
    kept = half_sum(part)
    block = kept.shape[0] // 2
    got = swap(kept[block:], "tensor", 2)
    return kept[:block].astype(jnp.float32) + got.astype(jnp.float32)


def both_halves(half):
    return jnp.concatenate([half, swap(half, "tensor", 1)], axis=0)


def butterfly(values):
    for axis in ("tensor", "dp"):
        mask = 1
        while mask < lax.axis_size(axis):
            values = values + swap(values, axis, mask)
            mask *= 2
    return values


def newton_schulz(square):
    bf16 = jnp.bfloat16
    size = square.shape[0]
    rows = lax.broadcasted_iota(jnp.int32, (size, size), 0)
    eye = rows == lax.broadcasted_iota(jnp.int32, (size, size), 1)
    product = None
    for index in range(NS_STEPS):
        mean = jnp.sum(jnp.where(eye, square, 0.0)) / size
        shift = square - jnp.where(eye, mean, 0.0)
        level = POLY_FIRST + POLY_SECOND * mean + POLY_THIRD * mean * mean
        slope = POLY_SECOND + 2.0 * POLY_THIRD * mean
        shift16 = shift.astype(bf16)
        rest = slope * shift + POLY_THIRD * dot(shift16, shift16)
        rest16 = rest.astype(bf16)
        if product is None:
            product = jnp.where(eye, level, 0.0) + rest
        else:
            product = level * product + dot(rest16, product.astype(bf16))
        if index < NS_STEPS - 1:
            wide = 2.0 * level * rest + dot(rest16, rest16)
            square = (
                jnp.where(eye, level * level * mean, 0.0)
                + level * level * shift
                + mean * wide
                + dot(wide.astype(bf16), shift16)
            )
    return product


def body(
    block_in,
    d_output,
    doc_ids,
    w_query,
    w_key,
    w_value,
    w_output,
    w_gate,
    w_up,
    w_down,
    mom_query,
    mom_key,
    mom_value,
    mom_output,
    mom_gate,
    mom_up,
    mom_down,
    gains,
    adam_first,
    adam_second,
):
    f32 = jnp.float32
    bf16 = jnp.bfloat16
    tensor_count = lax.axis_size("tensor")
    data_count = lax.axis_size("dp")
    my_data = lax.axis_index("dp")
    my_tensor = lax.axis_index("tensor")
    own = block_in.shape[0]
    model_width = block_in.shape[1]
    head_width = w_key.shape[1]
    hidden_width = w_gate.shape[1]
    seq_len = doc_ids.shape[1]
    assert tensor_count == 4 and doc_ids.shape[0] == 1 and w_query.shape[1] == head_width
    assert own * tensor_count == seq_len
    scale = head_width ** (-0.5)
    pre_attn = gains[0:model_width]
    post_attn = gains[model_width : 2 * model_width]
    pre_ffn = gains[2 * model_width : 3 * model_width]
    post_ffn = gains[3 * model_width : 4 * model_width]
    gain_q = gains[4 * model_width : 4 * model_width + head_width]
    gain_k = gains[4 * model_width + head_width :]

    order = (0, 2, 1, 3)

    weights_qkv = gather_data(
        jnp.concatenate([w_query, w_key, w_value], axis=1).astype(bf16)
    )
    weight_o = gather_data(w_output.astype(bf16))
    weights_gu = gather_data(jnp.concatenate([w_gate, w_up], axis=1).astype(bf16))
    weight_d = gather_data(w_down.astype(bf16))

    rows_in = jnp.concatenate([block_in, swap(block_in, "tensor", 2)], axis=0)
    normed_one = both_halves(rms_norm(rows_in, pre_attn).astype(bf16))
    cot_rows = jnp.concatenate([d_output, swap(d_output, "tensor", 2)], axis=0)

    doc_blocks = doc_ids.reshape(tensor_count, own)
    docs = jnp.concatenate(
        [lax.dynamic_index_in_dim(doc_blocks, my_tensor ^ j, 0, keepdims=False) for j in order]
    )
    places = jnp.concatenate(
        [(my_tensor ^ j) * own + jnp.arange(own, dtype=jnp.int32) for j in order]
    )
    first = jnp.sum((docs[None, :] < docs[:, None]).astype(jnp.int32), axis=-1)
    offset = (places - first).astype(f32)
    freqs = ROPE_BASE ** (-(2.0 * jnp.arange(head_width // 2, dtype=f32)) / head_width)
    angles = offset[:, None] * freqs
    cosine, sine = jnp.cos(angles), jnp.sin(angles)
    cosine = jnp.concatenate([cosine, cosine], axis=-1)
    sine = jnp.concatenate([sine, sine], axis=-1)
    allowed = (docs[None, :] == docs[:, None]) & (places[None, :] <= places[:, None])

    raw = dot(normed_one, weights_qkv)
    queries = raw[:, :head_width]
    keys = raw[:, head_width : 2 * head_width]
    values = raw[:, 2 * head_width :].astype(bf16)
    query_rot = rotate(rms_norm(queries, gain_q), cosine, sine).astype(bf16)
    key_rot = rotate(rms_norm(keys, gain_k), cosine, sine).astype(bf16)
    scores = jnp.where(allowed, dot_cols(query_rot, key_rot) * scale, MASKED)
    top = jnp.max(scores, axis=-1, keepdims=True)
    log_total = top + jnp.log(jnp.sum(jnp.exp(scores - top), axis=-1, keepdims=True))
    prob_full = jnp.exp(scores - log_total)
    probs = prob_full.astype(bf16)
    heads = dot(probs, values).astype(bf16)

    attn = row_sum(dot_cols(heads, weight_o))
    middle = rows_in + rms_norm(attn, post_attn)
    normed_two = both_halves(rms_norm(middle, pre_ffn).astype(bf16))
    gate_up = dot(normed_two, weights_gu)
    gate = gate_up[:, :hidden_width]
    upper = gate_up[:, hidden_width:]
    hidden = gated(gate, upper).astype(bf16)
    branch = row_sum(dot_cols(hidden, weight_d))
    block_out = middle[:own] + rms_norm(branch[:own], post_ffn)

    d_branch, g_post_ffn = rms_pull(branch, post_ffn, cot_rows)
    branch_low = both_halves(d_branch.astype(bf16))
    sum_down = scatter_data(dot_rows(branch_low, hidden))
    d_hidden = dot(branch_low, weight_d)
    d_gate, d_upper = jax.vjp(gated, gate, upper)[1](d_hidden)
    gu_low = jnp.concatenate([d_gate.astype(bf16), d_upper.astype(bf16)], axis=1)
    sum_gu = scatter_data(dot_rows(normed_two, gu_low))
    d_normed_two = row_sum(dot_cols(gu_low, weights_gu))
    d_mid_extra, g_pre_ffn = rms_pull(middle, pre_ffn, d_normed_two)
    d_middle = cot_rows + d_mid_extra
    d_attn, g_post_attn = rms_pull(attn, post_attn, d_middle)
    attn_low = both_halves(d_attn.astype(bf16))
    sum_output = scatter_data(dot_rows(attn_low, heads))

    d_heads = dot(attn_low, weight_o).astype(bf16)
    delta = jnp.sum(d_heads.astype(f32) * heads.astype(f32), axis=-1, keepdims=True)
    d_probs = dot_cols(d_heads, values)
    d_scores = (prob_full * (d_probs - delta) * scale).astype(bf16)
    d_qrot = dot(d_scores, key_rot)
    d_krot = dot_rows(d_scores, query_rot)
    d_vals = dot_rows(probs, d_heads)
    d_queries, g_query = rms_pull(queries, gain_q, rotate_back(d_qrot, cosine, sine))
    d_keys, g_key = rms_pull(keys, gain_k, rotate_back(d_krot, cosine, sine))
    qkv_low = jnp.concatenate(
        [d_queries.astype(bf16), d_keys.astype(bf16), d_vals.astype(bf16)], axis=1
    )
    query_low = qkv_low[:, :head_width]
    kv_low = qkv_low[:, head_width:]
    share = kv_low.shape[1] // tensor_count

    def quarter(mask):
        return lax.dynamic_slice_in_dim(kv_low, (my_tensor ^ mask) * share, share, 1)

    kv_total = quarter(0).astype(f32)
    for mask in range(1, tensor_count):
        got = swap(quarter(mask), "tensor", mask).reshape(tensor_count, own, share)
        got = jnp.concatenate([got[order.index(j ^ mask)] for j in order], axis=0)
        kv_total = kv_total + got.astype(f32)
    grad_qkv = jnp.concatenate(
        [dot_rows(normed_one, query_low), dot_rows(normed_one, kv_total.astype(bf16))], axis=1
    )
    sum_qkv = scatter_data(grad_qkv)
    sum_query = sum_qkv[:, :head_width]
    sum_kv = lax.all_gather(sum_qkv[:, head_width:], "tensor", axis=1, tiled=True)
    sum_key, sum_value = sum_kv[:, :head_width], sum_kv[:, head_width:]
    d_normed_one = row_sum_own(dot_cols(qkv_low, weights_qkv))
    d_in_extra, g_pre_attn = rms_pull(block_in, pre_attn, d_normed_one)
    d_input = d_middle[:own] + d_in_extra
    gain_term = jnp.concatenate(
        [
            jnp.sum(g_pre_attn, axis=0),
            jnp.sum(g_post_attn[:own], axis=0),
            jnp.sum(g_pre_ffn[:own], axis=0),
            jnp.sum(g_post_ffn[:own], axis=0),
            jnp.sum(g_query, axis=0),
            jnp.sum(g_key, axis=0),
        ]
    )
    grad_gains = butterfly(gain_term)
    sum_gate, sum_up = sum_gu[:, :hidden_width], sum_gu[:, hidden_width:]

    shard_rows = w_key.shape[0]
    weights = (w_query, w_key, w_value, w_output, w_gate, w_up, w_down)
    moments = (mom_query, mom_key, mom_value, mom_output, mom_gate, mom_up, mom_down)
    reduced = (sum_query, sum_key, sum_value, sum_output, sum_gate, sum_up, sum_down)
    whole_cols = [
        weights[index].shape[1] * (1 if index in (1, 2) else tensor_count) for index in range(7)
    ]
    slot = max([weight.shape[1] for weight in weights])
    owners = [index * data_count // 7 for index in range(7)]
    moved = [MUON_BETA * moments[index] + reduced[index] for index in range(7)]
    outgoing = jnp.zeros((data_count, shard_rows, slot), bf16)
    for index in range(7):
        push = (reduced[index] + MUON_BETA * moved[index]).astype(bf16)
        padded = jnp.pad(push, ((0, 0), (0, slot - push.shape[1])))
        outgoing = outgoing.at[owners[index]].set(padded)
    arrived = lax.all_to_all(outgoing, "dp", split_axis=0, concat_axis=0, tiled=True)
    owned = arrived.reshape(data_count * shard_rows, slot)
    turned = (my_data == owners[1]) | (my_data == owners[2])
    across = swap(owned, "tensor", 2)
    gram = dot_cols(owned, owned)
    near = swap(owned, "tensor", 1)
    gram = gram + dot_cols(near, near)
    gram = gram + dot_cols(across, across)
    far = swap(across, "tensor", 1)
    gram = gram + dot_cols(far, far)
    spare = model_width - slot
    gram = jnp.where(turned, jnp.pad(dot_rows(owned, owned), ((0, spare), (0, spare))), gram)
    size = gram.shape[0]
    eye = lax.broadcasted_iota(jnp.int32, (size, size), 0) == lax.broadcasted_iota(
        jnp.int32, (size, size), 1
    )
    norm_total = jnp.sum(jnp.where(eye, gram, 0.0))
    inverse = 1.0 / (jnp.sqrt(norm_total) + 1e-07)
    product = newton_schulz(gram * inverse * inverse).astype(bf16)
    ortho = jnp.where(turned, dot(owned, product[:slot, :slot]), dot(product, owned))
    ortho = (ortho * inverse).astype(bf16)
    returned = lax.all_to_all(
        ortho.reshape(data_count, shard_rows, slot), "dp", split_axis=0, concat_axis=0, tiled=True
    )
    updated = []
    for index in range(7):
        weight = weights[index]
        update = returned[owners[index], :, : weight.shape[1]].astype(f32)
        factor = 0.2 * math.sqrt(max(model_width, whole_cols[index]))
        updated.append(weight - MUON_RATE * (factor * update + MUON_DECAY * weight))
    next_first = FIRST_DECAY * adam_first + (1.0 - FIRST_DECAY) * grad_gains
    next_second = SECOND_DECAY * adam_second + (1.0 - SECOND_DECAY) * grad_gains * grad_gains
    first_fix = 1.0 - FIRST_DECAY**STEP
    second_fix = 1.0 - SECOND_DECAY**STEP
    new_gains = gains - ADAM_RATE * (next_first / first_fix) / (
        jnp.sqrt(next_second / second_fix) + ADAM_EPSILON
    )
    return (
        block_out,
        d_input,
        sum_query,
        sum_key,
        sum_value,
        sum_output,
        sum_gate,
        sum_up,
        sum_down,
        grad_gains,
        updated[0],
        updated[1],
        updated[2],
        updated[3],
        updated[4],
        updated[5],
        updated[6],
        moved[0],
        moved[1],
        moved[2],
        moved[3],
        moved[4],
        moved[5],
        moved[6],
        new_gains,
        next_first,
        next_second,
    )


def solution(mesh):
    return jax.shard_map(
        body,
        mesh=mesh,
        in_specs=(
            P(("dp", "tensor"), None),
            P(("dp", "tensor"), None),
            P("dp", None),
            P("dp", "tensor"),
            P("dp", None),
            P("dp", None),
            P("dp", "tensor"),
            P("dp", "tensor"),
            P("dp", "tensor"),
            P("dp", "tensor"),
            P("dp", "tensor"),
            P("dp", None),
            P("dp", None),
            P("dp", "tensor"),
            P("dp", "tensor"),
            P("dp", "tensor"),
            P("dp", "tensor"),
            P(),
            P(),
            P(),
        ),
        out_specs=(
            P(("dp", "tensor"), None),
            P(("dp", "tensor"), None),
            P("dp", "tensor"),
            P("dp", None),
            P("dp", None),
            P("dp", "tensor"),
            P("dp", "tensor"),
            P("dp", "tensor"),
            P("dp", "tensor"),
            P(),
            P("dp", "tensor"),
            P("dp", None),
            P("dp", None),
            P("dp", "tensor"),
            P("dp", "tensor"),
            P("dp", "tensor"),
            P("dp", "tensor"),
            P("dp", "tensor"),
            P("dp", None),
            P("dp", None),
            P("dp", "tensor"),
            P("dp", "tensor"),
            P("dp", "tensor"),
            P("dp", "tensor"),
            P(),
            P(),
            P(),
        ),
        check_vma=False,
    )
```

```python
import math

import jax
import jax.numpy as jnp
from jax import lax
from jax.experimental import pallas as pl
from jax.experimental.pallas import tpu as pltpu
from jax.sharding import Mesh
from jax.sharding import PartitionSpec as P

NS_STEPS = 5
STEP = 5


EPSILON = 1e-06
ROPE_BASE = 10000.0
MUON_BETA = 0.95
MUON_RATE = 0.04
MUON_DECAY = 0.1
POLY_FIRST = 3.4445
POLY_SECOND = -4.775
POLY_THIRD = 2.0315
FIRST_DECAY = 0.9
SECOND_DECAY = 0.95
ADAM_RATE = 0.05
ADAM_EPSILON = 1e-08
MASKED = -1e30


def rms_factor(values):
    return lax.rsqrt(jnp.mean(values * values, axis=-1, keepdims=True) + EPSILON)


def rms_norm(values, gain):
    return values * rms_factor(values) * (1.0 + gain)


def rms_pull(values, gain, cotangent):
    factor = rms_factor(values)
    scaled = cotangent * (1.0 + gain)
    inner = jnp.mean(values * scaled, axis=-1, keepdims=True)
    d_values = factor * scaled - values * (factor * factor * factor * inner)
    return d_values, cotangent * values * factor


def rotate(values, cosine, sine):
    half = values.shape[-1] // 2
    turned = jnp.concatenate([-values[..., half:], values[..., :half]], axis=-1)
    return values * cosine + turned * sine


def rotate_back(values, cosine, sine):
    half = values.shape[-1] // 2
    turned = values * sine
    turned = jnp.concatenate([turned[..., half:], -turned[..., :half]], axis=-1)
    return values * cosine + turned


def gated(gate, upper):
    return jax.nn.gelu(gate, approximate=True) * upper


def swap(values, axis, mask):
    count = lax.axis_size(axis)
    return lax.ppermute(values, axis, [(i, i ^ mask) for i in range(count)])


def dot(left, right):
    return jnp.dot(left, right, preferred_element_type=jnp.float32)


def dot_rows(left, right):
    return lax.dot_general(
        left, right, (((0,), (0,)), ((), ())), preferred_element_type=jnp.float32
    )


def dot_cols(left, right):
    return lax.dot_general(
        left, right, (((1,), (1,)), ((), ())), preferred_element_type=jnp.float32
    )


def half_sum(part):
    half = part.shape[0] // 2
    got = swap(part[half:].astype(jnp.bfloat16), "tensor", 1)
    return (part[:half] + got.astype(jnp.float32)).astype(jnp.bfloat16)


def row_sum(part):
    kept = half_sum(part)
    got = swap(kept, "tensor", 2)
    block = kept.shape[0] // 2
    got = jnp.concatenate([got[block:], got[:block]], axis=0)
    return kept.astype(jnp.float32) + got.astype(jnp.float32)


def row_sum_own(part):
    kept = half_sum(part)
    block = kept.shape[0] // 2
    got = swap(kept[block:], "tensor", 2)
    return kept[:block].astype(jnp.float32) + got.astype(jnp.float32)


def both_halves(half):
    return jnp.concatenate([half, swap(half, "tensor", 1)], axis=0)


DATA = ("major", "minor")


def exchange(values, axis):
    return lax.all_to_all(values, axis, split_axis=0, concat_axis=0, tiled=True)


def repeated(values, count):
    return jnp.broadcast_to(values[None], (count,) + values.shape)


def gather_major(block):
    return exchange(repeated(block, lax.axis_size("major")), "major")


def gather_minor(mine):
    other = swap(mine, "minor", 1)
    even = lax.axis_index("minor") == 0
    both = jnp.stack([jnp.where(even, mine, other), jnp.where(even, other, mine)], axis=1)
    return both.reshape(-1, mine.shape[-1])


def pair_sum(part):
    low = lax.axis_index("minor")
    rows = part.shape[0] // lax.axis_size(DATA)
    blocks = part.reshape(-1, 2, rows, part.shape[1])
    away = lax.dynamic_index_in_dim(blocks, 1 - low, 1, keepdims=False).astype(jnp.bfloat16)
    here = lax.dynamic_index_in_dim(blocks, low, 1, keepdims=False)
    return (here + swap(away, "minor", 1).astype(jnp.float32)).astype(jnp.bfloat16)


def butterfly(values, axes):
    for axis in axes:
        mask = 1
        while mask < lax.axis_size(axis):
            values = values + swap(values, axis, mask)
            mask *= 2
    return values


def total_of(blocks):
    return jnp.sum(blocks.astype(jnp.float32), axis=0)


def on_chip(math_fn, shapes, *operands, flags=None, fetch=False):
    if shapes[0].shape[-2] % 16:
        if flags is None:
            return math_fn(*operands)
        return math_fn(flags, *operands)

    def kernel(*refs):
        scalars = () if flags is None else (refs[0],)
        ins = refs[len(scalars) : len(scalars) + len(operands)]
        outs = refs[len(scalars) + len(operands) :][: len(shapes)]
        if fetch:
            held = refs[len(scalars) + len(operands) + len(shapes) : -1]
            copies = [
                pltpu.make_async_copy(ref, spot, refs[-1].at[index])
                for index, (ref, spot) in enumerate(zip(ins, held))
            ]
            for copy in copies:
                copy.start()
            for copy in copies:
                copy.wait()
            ins = held
        results = math_fn(*scalars, *[ref[...] for ref in ins])
        for out, result in zip(outs, results):
            out[...] = result

    space = pl.ANY if fetch else pltpu.VMEM
    specs = [pl.BlockSpec(memory_space=space)] * len(operands)
    scratch = []
    if fetch:
        scratch = [pltpu.VMEM(operand.shape, operand.dtype) for operand in operands]
        scratch.append(pltpu.SemaphoreType.DMA((len(operands),)))
    if flags is not None:
        specs = [pl.BlockSpec(memory_space=pltpu.SMEM)] + specs
        operands_all = (flags,) + operands
    else:
        operands_all = operands
    return pl.pallas_call(
        kernel,
        out_shape=tuple(shapes),
        in_specs=specs,
        out_specs=tuple([pl.BlockSpec(memory_space=pltpu.VMEM)] * len(shapes)),
        scratch_shapes=scratch,
    )(*operands_all)


def diagonal_mask(size):
    rows = lax.broadcasted_iota(jnp.int32, (size, size), 0)
    return rows == lax.broadcasted_iota(jnp.int32, (size, size), 1)


def newton_schulz(flags, owned, near, across, far, pair_width):
    f32 = jnp.float32
    bf16 = jnp.bfloat16
    size, slot = owned.shape

    def kernel(flag_ref, own_ref, near_ref, across_ref, far_ref, out_ref, gram, product, both, inv):
        turned = flag_ref[0] == 1

        @pl.when(jnp.logical_not(turned))
        def _():
            total = dot_cols(own_ref[...], own_ref[...])
            for ref in (near_ref, across_ref, far_ref):
                total = total + dot_cols(ref[...], ref[...])
            norm = jnp.sum(jnp.where(diagonal_mask(size), total, 0.0))
            inverse = 1.0 / (jnp.sqrt(jnp.full((1, slot), norm, f32)) + 1e-07)
            inv[...] = inverse
            gram[...] = total * (inverse[:, :1] * inverse[:, :1])

        @pl.when(turned)
        def _():
            total = own_ref[...].astype(f32)
            for ref in (near_ref, across_ref, far_ref):
                total = total + ref[...].astype(f32)
            joined = total.astype(bf16)
            both[...] = joined
            wide = joined.astype(f32)
            squares = jnp.sum(wide * wide, axis=0, keepdims=True)
            lane = lax.broadcasted_iota(jnp.int32, (1, slot), 1)
            left = jnp.sum(jnp.where(lane < pair_width, squares, 0.0))
            right = jnp.sum(jnp.where(lane < pair_width, 0.0, squares))
            norms = jnp.where(lane < pair_width, left, right)
            inverse = 1.0 / (jnp.sqrt(norms) + 1e-07)
            inv[...] = inverse
            square = dot_rows(joined, joined)
            rows = lax.broadcasted_iota(jnp.int32, (slot, slot), 0)
            cols = lax.broadcasted_iota(jnp.int32, (slot, slot), 1)
            same = (rows < pair_width) == (cols < pair_width)
            gram[...] = jnp.zeros((size, size), f32)
            gram[:slot, :slot] = jnp.where(same, square * (inverse * inverse), 0.0)

        product[...] = jnp.where(diagonal_mask(size), 1.0, 0.0)

        def step(index, carry):
            eye = diagonal_mask(size)
            square = gram[...]
            mean = jnp.sum(jnp.where(eye, square, 0.0)) / size
            shift = square - jnp.where(eye, mean, 0.0)
            level = POLY_FIRST + POLY_SECOND * mean + POLY_THIRD * mean * mean
            slope = POLY_SECOND + 2.0 * POLY_THIRD * mean
            shift16 = shift.astype(bf16)
            rest = slope * shift + POLY_THIRD * dot(shift16, shift16)
            rest16 = rest.astype(bf16)
            before = product[...]
            product[...] = level * before + dot(rest16, before.astype(bf16))

            @pl.when(index < NS_STEPS - 1)
            def _():
                wide = 2.0 * level * rest + dot(rest16, rest16)
                gram[...] = (
                    jnp.where(eye, level * level * mean, 0.0)
                    + level * level * shift
                    + mean * wide
                    + dot(wide.astype(bf16), shift16)
                )

            return carry

        lax.fori_loop(0, NS_STEPS, step, 0)
        narrow = product[...].astype(bf16)

        @pl.when(jnp.logical_not(turned))
        def _():
            out_ref[...] = (dot(narrow, own_ref[...]) * inv[...]).astype(bf16)

        @pl.when(turned)
        def _():
            out_ref[...] = (dot(both[...], narrow[:slot, :slot]) * inv[...]).astype(bf16)

    vmem = pl.BlockSpec(memory_space=pltpu.VMEM)
    return pl.pallas_call(
        kernel,
        out_shape=jax.ShapeDtypeStruct((size, slot), bf16),
        in_specs=[pl.BlockSpec(memory_space=pltpu.SMEM), vmem, vmem, vmem, vmem],
        out_specs=vmem,
        scratch_shapes=[
            pltpu.VMEM((size, size), f32),
            pltpu.VMEM((size, size), f32),
            pltpu.VMEM((size, slot), bf16),
            pltpu.VMEM((1, slot), f32),
        ],
        compiler_params=pltpu.CompilerParams(vmem_limit_bytes=24 * 1024 * 1024),
    )(flags, owned, near, across, far)


def body(
    block_in,
    d_output,
    doc_ids,
    w_query,
    w_key,
    w_value,
    w_output,
    w_gate,
    w_up,
    w_down,
    mom_query,
    mom_key,
    mom_value,
    mom_output,
    mom_gate,
    mom_up,
    mom_down,
    gains,
    adam_first,
    adam_second,
):
    f32 = jnp.float32
    bf16 = jnp.bfloat16
    tensor_count = lax.axis_size("tensor")
    data_count = lax.axis_size(DATA)
    my_data = lax.axis_index(DATA)
    my_tensor = lax.axis_index("tensor")
    own = block_in.shape[0]
    model_width = block_in.shape[1]
    head_width = w_key.shape[1]
    hidden_width = w_gate.shape[1]
    seq_len = doc_ids.shape[1]
    shard_rows = w_key.shape[0]
    assert tensor_count == 4 and doc_ids.shape[0] == 1 and w_query.shape[1] == head_width
    assert own * tensor_count == seq_len and hidden_width == 2 * head_width
    scale = head_width ** (-0.5)
    pre_attn = gains[0:model_width]
    post_attn = gains[model_width : 2 * model_width]
    pre_ffn = gains[2 * model_width : 3 * model_width]
    post_ffn = gains[3 * model_width : 4 * model_width]
    gain_q = gains[4 * model_width : 4 * model_width + head_width]
    gain_k = gains[4 * model_width + head_width :]
    first_core = (my_tensor & 1) == 0

    order = (0, 2, 1, 3)

    def pack(flags, query, key, value, output, gate, upper, down):
        half = jnp.where(flags[0] == 0, key, value)
        attn = jnp.concatenate([query, half, output], axis=1).astype(bf16)
        gate_up = jnp.concatenate([gate, upper], axis=1).astype(bf16)
        return repeated(attn, data_count), gate_up, down.astype(bf16)

    packed_attn, packed_gu, packed_d = on_chip(
        pack,
        [
            jax.ShapeDtypeStruct((data_count, shard_rows, 3 * head_width), bf16),
            jax.ShapeDtypeStruct((shard_rows, 2 * hidden_width), bf16),
            jax.ShapeDtypeStruct((shard_rows, hidden_width), bf16),
        ],
        w_query,
        w_key,
        w_value,
        w_output,
        w_gate,
        w_up,
        w_down,
        flags=(my_tensor & 1).reshape(1),
        fetch=True,
    )
    weights_attn = exchange(packed_attn, DATA).reshape(model_width, 3 * head_width)
    packed_gu, weights_attn = lax.optimization_barrier((packed_gu, weights_attn))
    major_gu = gather_major(packed_gu)
    packed_d, major_gu = lax.optimization_barrier((packed_d, major_gu))
    weights_gu = gather_minor(major_gu)
    major_d = gather_major(packed_d)
    weight_d = gather_minor(major_d)
    weight_q = weights_attn[:, :head_width]
    weight_half = weights_attn[:, head_width : 2 * head_width]
    weight_o = weights_attn[:, 2 * head_width :]
    weight_other = swap(weight_half, "tensor", 1)
    weights_qkv = jnp.concatenate(
        [
            weight_q,
            jnp.where(first_core, weight_half, weight_other),
            jnp.where(first_core, weight_other, weight_half),
        ],
        axis=1,
    )

    rows_in = jnp.concatenate([block_in, swap(block_in, "tensor", 2)], axis=0)
    normed_one = both_halves(rms_norm(rows_in, pre_attn).astype(bf16))
    cot_rows = jnp.concatenate([d_output, swap(d_output, "tensor", 2)], axis=0)
    normed_one, cot_rows = lax.optimization_barrier((normed_one, cot_rows))

    doc_blocks = doc_ids.reshape(tensor_count, own)
    docs = jnp.concatenate(
        [lax.dynamic_index_in_dim(doc_blocks, my_tensor ^ j, 0, keepdims=False) for j in order]
    )
    places = jnp.concatenate(
        [(my_tensor ^ j) * own + jnp.arange(own, dtype=jnp.int32) for j in order]
    )
    first = jnp.sum((docs[None, :] < docs[:, None]).astype(jnp.int32), axis=-1)
    offset = (places - first).astype(f32)
    freqs = ROPE_BASE ** (-(2.0 * jnp.arange(head_width // 2, dtype=f32)) / head_width)
    angles = offset[:, None] * freqs
    cosine, sine = jnp.cos(angles), jnp.sin(angles)
    cosine = jnp.concatenate([cosine, cosine], axis=-1)
    sine = jnp.concatenate([sine, sine], axis=-1)
    allowed = (docs[None, :] == docs[:, None]) & (places[None, :] <= places[:, None])

    raw = dot(normed_one, weights_qkv)
    queries = raw[:, :head_width]
    keys = raw[:, head_width : 2 * head_width]
    values = raw[:, 2 * head_width :].astype(bf16)
    query_rot = rotate(rms_norm(queries, gain_q), cosine, sine).astype(bf16)
    key_rot = rotate(rms_norm(keys, gain_k), cosine, sine).astype(bf16)
    scores = jnp.where(allowed, dot_cols(query_rot, key_rot) * scale, MASKED)
    top = jnp.max(scores, axis=-1, keepdims=True)
    log_total = top + jnp.log(jnp.sum(jnp.exp(scores - top), axis=-1, keepdims=True))
    prob_full = jnp.exp(scores - log_total)
    probs = prob_full.astype(bf16)
    heads = dot(probs, values).astype(bf16)

    attn = row_sum(dot_cols(heads, weight_o))
    middle = rows_in + rms_norm(attn, post_attn)
    normed_two = both_halves(rms_norm(middle, pre_ffn).astype(bf16))
    gate_up = dot(normed_two, weights_gu)
    gate = gate_up[:, :hidden_width]
    upper = gate_up[:, hidden_width:]
    hidden = gated(gate, upper).astype(bf16)
    branch = row_sum(dot_cols(hidden, weight_d))
    block_out = middle[:own] + rms_norm(branch[:own], post_ffn)

    d_branch, g_post_ffn = rms_pull(branch, post_ffn, cot_rows)
    branch_low = both_halves(d_branch.astype(bf16))
    pair_d = pair_sum(dot_rows(branch_low, hidden))
    arrived_d = exchange(pair_d, "major")
    d_hidden = dot(branch_low, weight_d)
    d_gate, d_upper = jax.vjp(gated, gate, upper)[1](d_hidden)
    gu_low = jnp.concatenate([d_gate.astype(bf16), d_upper.astype(bf16)], axis=1)
    pair_gu = pair_sum(dot_rows(normed_two, gu_low))
    pair_gu, arrived_d = lax.optimization_barrier((pair_gu, arrived_d))
    arrived_gu = exchange(pair_gu, "major")
    d_normed_two = row_sum(dot_cols(gu_low, weights_gu))
    d_mid_extra, g_pre_ffn = rms_pull(middle, pre_ffn, d_normed_two)
    d_middle = cot_rows + d_mid_extra
    d_attn, g_post_attn = rms_pull(attn, post_attn, d_middle)
    attn_low = both_halves(d_attn.astype(bf16))
    grad_o = dot_rows(attn_low, heads).astype(bf16)

    d_heads = dot(attn_low, weight_o).astype(bf16)
    delta = jnp.sum(d_heads.astype(f32) * heads.astype(f32), axis=-1, keepdims=True)
    d_probs = dot_cols(d_heads, values)
    d_scores = (prob_full * (d_probs - delta) * scale).astype(bf16)
    d_qrot = dot(d_scores, key_rot)
    d_krot = dot_rows(d_scores, query_rot)
    d_vals = dot_rows(probs, d_heads)
    d_queries, g_query = rms_pull(queries, gain_q, rotate_back(d_qrot, cosine, sine))
    d_keys, g_key = rms_pull(keys, gain_k, rotate_back(d_krot, cosine, sine))
    qkv_low = jnp.concatenate(
        [d_queries.astype(bf16), d_keys.astype(bf16), d_vals.astype(bf16)], axis=1
    )
    grad_qkv = dot_rows(normed_one, qkv_low).astype(bf16)
    grad_attn = jnp.concatenate([grad_qkv, grad_o], axis=1)
    grad_attn, arrived_gu = lax.optimization_barrier((grad_attn, arrived_gu))
    arrived_attn = exchange(grad_attn.reshape(data_count, shard_rows, -1), DATA)

    d_normed_one = row_sum_own(dot_cols(qkv_low, weights_qkv))
    d_in_extra, g_pre_attn = rms_pull(block_in, pre_attn, d_normed_one)
    d_input = d_middle[:own] + d_in_extra
    gain_term = jnp.concatenate(
        [
            jnp.sum(g_pre_attn, axis=0),
            jnp.sum(g_post_attn[:own], axis=0),
            jnp.sum(g_pre_ffn[:own], axis=0),
            jnp.sum(g_post_ffn[:own], axis=0),
            jnp.sum(g_query, axis=0),
            jnp.sum(g_key, axis=0),
        ]
    )

    slot = hidden_width
    owners = [index * data_count // 6 for index in range(6)]

    def advance(flags, moved_d, moved_gu, moved_attn, *moments):
        m_query, m_key, m_value, m_output, m_gate, m_up, m_down = moments
        low = total_of(moved_attn)
        wide = total_of(moved_gu)
        terms = (
            low[:, :head_width],
            low[:, head_width : 3 * head_width],
            low[:, 3 * head_width :],
            wide[:, :hidden_width],
            wide[:, hidden_width:],
            total_of(moved_d),
        )
        share = jnp.where(flags[0] == 0, 1.0, 0.0)
        held = (
            m_query,
            jnp.concatenate([m_key, m_value], axis=1) * share,
            m_output,
            m_gate,
            m_up,
            m_down,
        )
        moved = [MUON_BETA * moment + term for moment, term in zip(held, terms)]
        blocks = []
        for index in range(data_count):
            if index not in owners:
                blocks.append(jnp.zeros((shard_rows, slot), bf16))
                continue
            which = owners.index(index)
            push = (terms[which] + MUON_BETA * moved[which]).astype(bf16)
            if push.shape[1] < slot:
                empty = jnp.zeros((shard_rows, slot - push.shape[1]), bf16)
                push = jnp.concatenate([push, empty], axis=1)
            blocks.append(push)
        keep = (0, 2, 3, 4, 5)
        return (
            (jnp.stack(blocks),)
            + tuple(terms)
            + tuple(moved[index] for index in keep)
        )

    def rows_of(width):
        return jax.ShapeDtypeStruct((shard_rows, width), f32)

    widths = (head_width, 2 * head_width, head_width, hidden_width, hidden_width, hidden_width)
    made = on_chip(
        advance,
        [jax.ShapeDtypeStruct((data_count, shard_rows, slot), bf16)]
        + [rows_of(width) for width in widths]
        + [rows_of(widths[index]) for index in (0, 2, 3, 4, 5)],
        arrived_d,
        arrived_gu,
        arrived_attn,
        mom_query,
        mom_key,
        mom_value,
        mom_output,
        mom_gate,
        mom_up,
        mom_down,
        flags=my_tensor.reshape(1),
        fetch=True,
    )
    outgoing, sum_query, part_kv, sum_output, sum_gate, sum_up, sum_down = made[:7]
    moved_query, moved_output, moved_gate, moved_up, moved_down = made[7:]

    owned = exchange(outgoing, DATA).reshape(data_count * shard_rows, slot)

    sum_kv = part_kv + swap(part_kv, "tensor", 1)
    sum_kv = sum_kv + swap(sum_kv, "tensor", 2)
    sum_key, sum_value = sum_kv[:, :head_width], sum_kv[:, head_width:]
    moved_key = MUON_BETA * mom_key + sum_key
    moved_value = MUON_BETA * mom_value + sum_value
    gain_half = butterfly(gain_term, ("tensor",))
    owned, gain_half, d_input = lax.optimization_barrier((owned, gain_half, d_input))
    across = swap(owned, "tensor", 2)
    grad_gains = butterfly(gain_half, ("minor", "major"))
    across, grad_gains = lax.optimization_barrier((across, grad_gains))
    near = swap(owned, "tensor", 1)
    far = swap(across, "tensor", 1)
    turned = (my_data == owners[1]).astype(jnp.int32).reshape(1)
    ortho = newton_schulz(turned, owned, near, across, far, head_width)
    returned = exchange(ortho.reshape(data_count, shard_rows, slot), DATA)

    weights = (w_query, w_key, w_value, w_output, w_gate, w_up, w_down)
    whole_cols = [
        weights[index].shape[1] * (1 if index in (1, 2) else tensor_count) for index in range(7)
    ]
    places_of = ((0, 0), (1, 0), (1, head_width), (2, 0), (3, 0), (4, 0), (5, 0))

    def renew(back, *held):
        results = []
        for index, weight in enumerate(held):
            which, start = places_of[index]
            update = back[owners[which]][:, start : start + weight.shape[1]].astype(f32)
            factor = 0.2 * math.sqrt(max(model_width, whole_cols[index]))
            results.append(weight - MUON_RATE * (factor * update + MUON_DECAY * weight))
        return tuple(results)

    updated = on_chip(
        renew, [rows_of(weight.shape[1]) for weight in weights], returned, *weights, fetch=True
    )
    next_first = FIRST_DECAY * adam_first + (1.0 - FIRST_DECAY) * grad_gains
    next_second = SECOND_DECAY * adam_second + (1.0 - SECOND_DECAY) * grad_gains * grad_gains
    first_fix = 1.0 - FIRST_DECAY**STEP
    second_fix = 1.0 - SECOND_DECAY**STEP
    new_gains = gains - ADAM_RATE * (next_first / first_fix) / (
        jnp.sqrt(next_second / second_fix) + ADAM_EPSILON
    )
    return (
        block_out,
        d_input,
        sum_query,
        sum_key,
        sum_value,
        sum_output,
        sum_gate,
        sum_up,
        sum_down,
        grad_gains,
        *updated,
        moved_query,
        moved_key,
        moved_value,
        moved_output,
        moved_gate,
        moved_up,
        moved_down,
        new_gains,
        next_first,
        next_second,
    )


def solution(mesh):
    tensor_count = mesh.shape["tensor"]
    split = Mesh(
        mesh.devices.reshape(-1, 2, tensor_count), ("major", "minor", "tensor")
    )
    rows = P(("major", "minor", "tensor"), None)
    both = P(DATA, "tensor")
    data = P(DATA, None)
    matrices = (both, data, data, both, both, both, both)

    return jax.shard_map(
        body,
        mesh=split,
        in_specs=(rows, rows, data) + matrices + matrices + (P(), P(), P()),
        out_specs=(rows, rows) + matrices + (P(),) + matrices + matrices + (P(), P(), P()),
        check_vma=False,
    )
```

```python
import math

import jax
import jax.numpy as jnp
from jax import lax
from jax.experimental import pallas as pl
from jax.experimental.pallas import tpu as pltpu
from jax.sharding import Mesh
from jax.sharding import PartitionSpec as P

NS_STEPS = 5
STEP = 5


EPSILON = 1e-06
ROPE_BASE = 10000.0
MUON_BETA = 0.95
MUON_RATE = 0.04
MUON_DECAY = 0.1
POLY_FIRST = 3.4445
POLY_SECOND = -4.775
POLY_THIRD = 2.0315
FIRST_DECAY = 0.9
SECOND_DECAY = 0.95
ADAM_RATE = 0.05
ADAM_EPSILON = 1e-08
MASKED = -1e30


def rms_factor(values):
    return lax.rsqrt(jnp.mean(values * values, axis=-1, keepdims=True) + EPSILON)


def rms_norm(values, gain):
    return values * rms_factor(values) * (1.0 + gain)


def rms_pull(values, gain, cotangent):
    factor = rms_factor(values)
    scaled = cotangent * (1.0 + gain)
    inner = jnp.mean(values * scaled, axis=-1, keepdims=True)
    d_values = factor * scaled - values * (factor * factor * factor * inner)
    return d_values, cotangent * values * factor


def rotate(values, cosine, sine):
    half = values.shape[-1] // 2
    turned = jnp.concatenate([-values[..., half:], values[..., :half]], axis=-1)
    return values * cosine + turned * sine


def rotate_back(values, cosine, sine):
    half = values.shape[-1] // 2
    turned = values * sine
    turned = jnp.concatenate([turned[..., half:], -turned[..., :half]], axis=-1)
    return values * cosine + turned


def gated(gate, upper):
    return jax.nn.gelu(gate, approximate=True) * upper


def swap(values, axis, mask):
    count = lax.axis_size(axis)
    return lax.ppermute(values, axis, [(i, i ^ mask) for i in range(count)])


def dot(left, right):
    return jnp.dot(left, right, preferred_element_type=jnp.float32)


def dot_rows(left, right):
    return lax.dot_general(
        left, right, (((0,), (0,)), ((), ())), preferred_element_type=jnp.float32
    )


def dot_cols(left, right):
    return lax.dot_general(
        left, right, (((1,), (1,)), ((), ())), preferred_element_type=jnp.float32
    )


def half_sum(part):
    half = part.shape[0] // 2
    got = swap(part[half:].astype(jnp.bfloat16), "tensor", 1)
    return (part[:half] + got.astype(jnp.float32)).astype(jnp.bfloat16)


def row_sum(part):
    kept = half_sum(part)
    got = swap(kept, "tensor", 2)
    block = kept.shape[0] // 2
    got = jnp.concatenate([got[block:], got[:block]], axis=0)
    return kept.astype(jnp.float32) + got.astype(jnp.float32)


def row_sum_own(part):
    kept = half_sum(part)
    block = kept.shape[0] // 2
    got = swap(kept[block:], "tensor", 2)
    return kept[:block].astype(jnp.float32) + got.astype(jnp.float32)


def both_halves(half):
    return jnp.concatenate([half, swap(half, "tensor", 1)], axis=0)


DATA = ("major", "minor")


def exchange(values, axis):
    return lax.all_to_all(values, axis, split_axis=0, concat_axis=0, tiled=True)


def repeated(values, count):
    return jnp.broadcast_to(values[None], (count,) + values.shape)


def gather_minor(mine):
    other = swap(mine, "minor", 1)
    even = lax.axis_index("minor") == 0
    both = jnp.stack([jnp.where(even, mine, other), jnp.where(even, other, mine)], axis=1)
    return both.reshape(-1, mine.shape[-1])


def pair_sum(part):
    low = lax.axis_index("minor")
    rows = part.shape[0] // lax.axis_size(DATA)
    blocks = part.reshape(-1, 2, rows, part.shape[1])
    away = swap(lax.dynamic_index_in_dim(blocks, 1 - low, 1, keepdims=False), "minor", 1)
    here = lax.dynamic_index_in_dim(blocks, low, 1, keepdims=False)
    return (here.astype(jnp.float32) + away.astype(jnp.float32)).astype(jnp.bfloat16)


def butterfly(values, axes):
    for axis in axes:
        mask = 1
        while mask < lax.axis_size(axis):
            values = values + swap(values, axis, mask)
            mask *= 2
    return values


def total_of(blocks):
    return jnp.sum(blocks.astype(jnp.float32), axis=0)


def on_chip(math_fn, shapes, *operands, flags=None, fetch=None, limit=None):
    if shapes[0].shape[-2] % 16:
        if flags is None:
            return math_fn(*operands)
        return math_fn(flags, *operands)

    def kernel(*refs):
        scalars = () if flags is None else (refs[0],)
        ins = refs[len(scalars) : len(scalars) + len(operands)]
        outs = refs[len(scalars) + len(operands) :][: len(shapes)]
        if fetch is not None:
            held = refs[len(scalars) + len(operands) + len(shapes) : -1]
            copies = [
                pltpu.make_async_copy(ref, spot, refs[-1].at[index])
                for index, (ref, spot) in enumerate(zip(ins[fetch:], held))
            ]
            for copy in copies:
                copy.start()
            for copy in copies:
                copy.wait()
            ins = ins[:fetch] + held
        results = math_fn(*scalars, *[ref[...] for ref in ins])
        for out, result in zip(outs, results):
            out[...] = result

    specs = [pl.BlockSpec(memory_space=pltpu.VMEM)] * len(operands)
    scratch = []
    if fetch is not None:
        specs[fetch:] = [pl.BlockSpec(memory_space=pl.ANY)] * (len(operands) - fetch)
        scratch = [pltpu.VMEM(operand.shape, operand.dtype) for operand in operands[fetch:]]
        scratch.append(pltpu.SemaphoreType.DMA((len(operands) - fetch,)))
    if flags is not None:
        specs = [pl.BlockSpec(memory_space=pltpu.SMEM)] + specs
        operands_all = (flags,) + operands
    else:
        operands_all = operands
    return pl.pallas_call(
        kernel,
        out_shape=tuple(shapes),
        in_specs=specs,
        out_specs=tuple([pl.BlockSpec(memory_space=pltpu.VMEM)] * len(shapes)),
        scratch_shapes=scratch,
        compiler_params=pltpu.CompilerParams(vmem_limit_bytes=limit),
    )(*operands_all)


def diagonal_mask(size):
    rows = lax.broadcasted_iota(jnp.int32, (size, size), 0)
    return rows == lax.broadcasted_iota(jnp.int32, (size, size), 1)


def newton_schulz(flags, owned, near, across, far, pair_width):
    f32 = jnp.float32
    bf16 = jnp.bfloat16
    size, slot = owned.shape

    def kernel(flag_ref, own_ref, near_ref, across_ref, far_ref, out_ref, gram, product, both, inv):
        turned = flag_ref[0] == 1

        @pl.when(jnp.logical_not(turned))
        def _():
            total = dot_cols(own_ref[...], own_ref[...])
            for ref in (near_ref, across_ref, far_ref):
                total = total + dot_cols(ref[...], ref[...])
            norm = jnp.sum(jnp.where(diagonal_mask(size), total, 0.0))
            inverse = 1.0 / (jnp.sqrt(jnp.full((1, slot), norm, f32)) + 1e-07)
            inv[...] = inverse
            gram[...] = total * (inverse[:, :1] * inverse[:, :1])

        @pl.when(turned)
        def _():
            total = own_ref[...].astype(f32)
            for ref in (near_ref, across_ref, far_ref):
                total = total + ref[...].astype(f32)
            joined = total.astype(bf16)
            both[...] = joined
            wide = joined.astype(f32)
            squares = jnp.sum(wide * wide, axis=0, keepdims=True)
            lane = lax.broadcasted_iota(jnp.int32, (1, slot), 1)
            left = jnp.sum(jnp.where(lane < pair_width, squares, 0.0))
            right = jnp.sum(jnp.where(lane < pair_width, 0.0, squares))
            norms = jnp.where(lane < pair_width, left, right)
            inverse = 1.0 / (jnp.sqrt(norms) + 1e-07)
            inv[...] = inverse
            square = dot_rows(joined, joined)
            rows = lax.broadcasted_iota(jnp.int32, (slot, slot), 0)
            cols = lax.broadcasted_iota(jnp.int32, (slot, slot), 1)
            same = (rows < pair_width) == (cols < pair_width)
            gram[...] = jnp.zeros((size, size), f32)
            gram[:slot, :slot] = jnp.where(same, square * (inverse * inverse), 0.0)

        def step(index, carry):
            eye = diagonal_mask(size)
            square = gram[...]
            mean = jnp.sum(jnp.where(eye, square, 0.0)) / size
            shift = square - jnp.where(eye, mean, 0.0)
            level = POLY_FIRST + POLY_SECOND * mean + POLY_THIRD * mean * mean
            slope = POLY_SECOND + 2.0 * POLY_THIRD * mean
            shift16 = shift.astype(bf16)
            rest = slope * shift + POLY_THIRD * dot(shift16, shift16)
            rest16 = rest.astype(bf16)

            @pl.when(index == 0)
            def _():
                product[...] = jnp.where(eye, level, 0.0) + rest

            @pl.when(index > 0)
            def _():
                before = product[...]
                product[...] = level * before + dot(rest16, before.astype(bf16))

            @pl.when(index < NS_STEPS - 1)
            def _():
                wide = 2.0 * level * rest + dot(rest16, rest16)
                gram[...] = (
                    jnp.where(eye, level * level * mean, 0.0)
                    + level * level * shift
                    + mean * wide
                    + dot(wide.astype(bf16), shift16)
                )

            return carry

        lax.fori_loop(0, NS_STEPS, step, 0)
        narrow = product[...].astype(bf16)

        @pl.when(jnp.logical_not(turned))
        def _():
            out_ref[...] = (dot(narrow, own_ref[...]) * inv[...]).astype(bf16)

        @pl.when(turned)
        def _():
            out_ref[...] = (dot(both[...], narrow[:slot, :slot]) * inv[...]).astype(bf16)

    vmem = pl.BlockSpec(memory_space=pltpu.VMEM)
    return pl.pallas_call(
        kernel,
        out_shape=jax.ShapeDtypeStruct((size, slot), bf16),
        in_specs=[pl.BlockSpec(memory_space=pltpu.SMEM), vmem, vmem, vmem, vmem],
        out_specs=vmem,
        scratch_shapes=[
            pltpu.VMEM((size, size), f32),
            pltpu.VMEM((size, size), f32),
            pltpu.VMEM((size, slot), bf16),
            pltpu.VMEM((1, slot), f32),
        ],
        compiler_params=pltpu.CompilerParams(vmem_limit_bytes=24 * 1024 * 1024),
    )(flags, owned, near, across, far)


def body(
    block_in,
    d_output,
    doc_ids,
    w_query,
    w_key,
    w_value,
    w_output,
    w_gate,
    w_up,
    w_down,
    mom_query,
    mom_key,
    mom_value,
    mom_output,
    mom_gate,
    mom_up,
    mom_down,
    gains,
    adam_first,
    adam_second,
):
    f32 = jnp.float32
    bf16 = jnp.bfloat16
    tensor_count = lax.axis_size("tensor")
    data_count = lax.axis_size(DATA)
    major_count = lax.axis_size("major")
    my_data = lax.axis_index(DATA)
    my_tensor = lax.axis_index("tensor")
    own = block_in.shape[0]
    model_width = block_in.shape[1]
    head_width = w_key.shape[1]
    hidden_width = w_gate.shape[1]
    seq_len = doc_ids.shape[1]
    shard_rows = w_key.shape[0]
    assert tensor_count == 4 and doc_ids.shape[0] == 1 and w_query.shape[1] == head_width
    assert own * tensor_count == seq_len and hidden_width == 2 * head_width
    scale = head_width ** (-0.5)
    pre_attn = gains[0:model_width]
    post_attn = gains[model_width : 2 * model_width]
    pre_ffn = gains[2 * model_width : 3 * model_width]
    post_ffn = gains[3 * model_width : 4 * model_width]
    gain_q = gains[4 * model_width : 4 * model_width + head_width]
    gain_k = gains[4 * model_width + head_width :]
    first_core = (my_tensor & 1) == 0

    order = (0, 2, 1, 3)

    def pack(flags, query, key, value, output, gate, upper, down):
        half = jnp.where(flags[0] == 0, key, value)
        attn = jnp.concatenate([query, half, output], axis=1).astype(bf16)
        gate_up = jnp.concatenate([gate, upper], axis=1).astype(bf16)
        return (
            repeated(attn, data_count),
            repeated(gate_up, major_count),
            repeated(down.astype(bf16), major_count),
        )

    packed_attn, packed_gu, packed_d = on_chip(
        pack,
        [
            jax.ShapeDtypeStruct((data_count, shard_rows, 3 * head_width), bf16),
            jax.ShapeDtypeStruct((major_count, shard_rows, 2 * hidden_width), bf16),
            jax.ShapeDtypeStruct((major_count, shard_rows, hidden_width), bf16),
        ],
        w_query,
        w_key,
        w_value,
        w_output,
        w_gate,
        w_up,
        w_down,
        flags=(my_tensor & 1).reshape(1),
        fetch=0,
    )
    weights_attn = exchange(packed_attn, DATA).reshape(model_width, 3 * head_width)
    packed_gu, weights_attn = lax.optimization_barrier((packed_gu, weights_attn))
    major_gu = exchange(packed_gu, "major")
    packed_d, major_gu = lax.optimization_barrier((packed_d, major_gu))
    weights_gu = gather_minor(major_gu)
    major_d = exchange(packed_d, "major")
    weight_d = gather_minor(major_d)
    weight_q = weights_attn[:, :head_width]
    weight_half = weights_attn[:, head_width : 2 * head_width]
    weight_o = weights_attn[:, 2 * head_width :]
    weight_other = swap(weight_half, "tensor", 1)
    weights_qkv = jnp.concatenate(
        [
            weight_q,
            jnp.where(first_core, weight_half, weight_other),
            jnp.where(first_core, weight_other, weight_half),
        ],
        axis=1,
    )

    rows_in = jnp.concatenate([block_in, swap(block_in, "tensor", 2)], axis=0)
    normed_one = both_halves(rms_norm(rows_in, pre_attn).astype(bf16))
    cot_rows = jnp.concatenate([d_output, swap(d_output, "tensor", 2)], axis=0)
    normed_one, cot_rows = lax.optimization_barrier((normed_one, cot_rows))

    doc_blocks = doc_ids.reshape(tensor_count, own)
    docs = jnp.concatenate(
        [lax.dynamic_index_in_dim(doc_blocks, my_tensor ^ j, 0, keepdims=False) for j in order]
    )
    places = jnp.concatenate(
        [(my_tensor ^ j) * own + jnp.arange(own, dtype=jnp.int32) for j in order]
    )
    first = jnp.sum((docs[None, :] < docs[:, None]).astype(jnp.int32), axis=-1)
    offset = (places - first).astype(f32)
    freqs = ROPE_BASE ** (-(2.0 * jnp.arange(head_width // 2, dtype=f32)) / head_width)
    angles = offset[:, None] * freqs
    cosine, sine = jnp.cos(angles), jnp.sin(angles)
    cosine = jnp.concatenate([cosine, cosine], axis=-1)
    sine = jnp.concatenate([sine, sine], axis=-1)
    allowed = (docs[None, :] == docs[:, None]) & (places[None, :] <= places[:, None])

    raw = dot(normed_one, weights_qkv)
    queries = raw[:, :head_width]
    keys = raw[:, head_width : 2 * head_width]
    values = raw[:, 2 * head_width :].astype(bf16)
    query_rot = rotate(rms_norm(queries, gain_q), cosine, sine).astype(bf16)
    key_rot = rotate(rms_norm(keys, gain_k), cosine, sine).astype(bf16)
    scores = jnp.where(allowed, dot_cols(query_rot, key_rot) * scale, MASKED)
    top = jnp.max(scores, axis=-1, keepdims=True)
    log_total = top + jnp.log(jnp.sum(jnp.exp(scores - top), axis=-1, keepdims=True))
    prob_full = jnp.exp(scores - log_total)
    probs = prob_full.astype(bf16)
    heads = dot(probs, values).astype(bf16)

    attn = row_sum(dot_cols(heads, weight_o))
    middle = rows_in + rms_norm(attn, post_attn)
    normed_two = both_halves(rms_norm(middle, pre_ffn).astype(bf16))
    gate_up = dot(normed_two, weights_gu)
    gate = gate_up[:, :hidden_width]
    upper = gate_up[:, hidden_width:]
    hidden = gated(gate, upper).astype(bf16)
    branch = row_sum(dot_cols(hidden, weight_d))
    block_out = middle[:own] + rms_norm(branch[:own], post_ffn)

    d_branch, g_post_ffn = rms_pull(branch, post_ffn, cot_rows)
    branch_low = both_halves(d_branch.astype(bf16))
    pair_d = pair_sum(dot_rows(branch_low, hidden).astype(bf16))
    arrived_d = exchange(pair_d, "major")
    d_hidden = dot(branch_low, weight_d)
    d_gate, d_upper = jax.vjp(gated, gate, upper)[1](d_hidden)
    gu_low = jnp.concatenate([d_gate.astype(bf16), d_upper.astype(bf16)], axis=1)
    pair_gu = pair_sum(dot_rows(normed_two, gu_low).astype(bf16))
    pair_gu, arrived_d = lax.optimization_barrier((pair_gu, arrived_d))
    arrived_gu = exchange(pair_gu, "major")
    d_normed_two = row_sum(dot_cols(gu_low, weights_gu))
    d_mid_extra, g_pre_ffn = rms_pull(middle, pre_ffn, d_normed_two)
    d_middle = cot_rows + d_mid_extra
    d_attn, g_post_attn = rms_pull(attn, post_attn, d_middle)
    attn_low = both_halves(d_attn.astype(bf16))
    grad_o = dot_rows(attn_low, heads).astype(bf16)

    d_heads = dot(attn_low, weight_o).astype(bf16)
    delta = jnp.sum(d_heads.astype(f32) * heads.astype(f32), axis=-1, keepdims=True)
    d_probs = dot_cols(d_heads, values)
    d_scores = (prob_full * (d_probs - delta) * scale).astype(bf16)
    d_qrot = dot(d_scores, key_rot)
    d_krot = dot_rows(d_scores, query_rot)
    d_vals = dot_rows(probs, d_heads)
    d_queries, g_query = rms_pull(queries, gain_q, rotate_back(d_qrot, cosine, sine))
    d_keys, g_key = rms_pull(keys, gain_k, rotate_back(d_krot, cosine, sine))
    qkv_low = jnp.concatenate(
        [d_queries.astype(bf16), d_keys.astype(bf16), d_vals.astype(bf16)], axis=1
    )
    grad_kv = dot_rows(normed_one, qkv_low[:, head_width:])
    grad_key, grad_value = grad_kv[:, :head_width], grad_kv[:, head_width:]
    got = swap(jnp.where(first_core, grad_value, grad_key).astype(bf16), "tensor", 1)
    grad_half = jnp.where(first_core, grad_key, grad_value) + got.astype(f32)
    grad_query = dot_rows(normed_one, qkv_low[:, :head_width])
    grad_attn = jnp.concatenate(
        [grad_query.astype(bf16), grad_half.astype(bf16), grad_o], axis=1
    )
    grad_attn, arrived_gu = lax.optimization_barrier((grad_attn, arrived_gu))
    arrived_attn = exchange(grad_attn.reshape(data_count, shard_rows, -1), DATA)

    d_normed_one = row_sum_own(dot_cols(qkv_low, weights_qkv))
    d_in_extra, g_pre_attn = rms_pull(block_in, pre_attn, d_normed_one)
    d_input = d_middle[:own] + d_in_extra
    gain_term = jnp.concatenate(
        [
            jnp.sum(g_pre_attn, axis=0),
            jnp.sum(g_post_attn[:own], axis=0),
            jnp.sum(g_pre_ffn[:own], axis=0),
            jnp.sum(g_post_ffn[:own], axis=0),
            jnp.sum(g_query, axis=0),
            jnp.sum(g_key, axis=0),
        ]
    )

    slot = hidden_width
    owners = [index * data_count // 6 for index in range(6)]

    def advance(flags, moved_d, moved_gu, moved_attn, *moments):
        m_query, m_key, m_value, m_output, m_gate, m_up, m_down = moments
        low = total_of(moved_attn)
        wide = total_of(moved_gu)
        terms = (
            low[:, :head_width],
            low[:, head_width : 2 * head_width],
            low[:, 2 * head_width :],
            wide[:, :hidden_width],
            wide[:, hidden_width:],
            total_of(moved_d),
        )
        share = jnp.where(flags[0] < 2, 1.0, 0.0)
        even = flags[0] % 2 == 0
        held = (
            m_query,
            jnp.where(even, m_key, m_value) * share,
            m_output,
            m_gate,
            m_up,
            m_down,
        )
        moved = [MUON_BETA * moment + term for moment, term in zip(held, terms)]
        blocks = []
        for index in range(data_count):
            if index not in owners:
                blocks.append(jnp.zeros((shard_rows, slot), bf16))
                continue
            which = owners.index(index)
            push = (terms[which] + MUON_BETA * moved[which]).astype(bf16)
            if which == 1:
                none = jnp.zeros_like(push)
                push = jnp.concatenate(
                    [jnp.where(even, push, none), jnp.where(even, none, push)], axis=1
                )
            if push.shape[1] < slot:
                empty = jnp.zeros((shard_rows, slot - push.shape[1]), bf16)
                push = jnp.concatenate([push, empty], axis=1)
            blocks.append(push)
        keep = (0, 2, 3, 4, 5)
        return (
            (jnp.stack(blocks),)
            + tuple(terms)
            + tuple(moved[index] for index in keep)
        )

    def rows_of(width):
        return jax.ShapeDtypeStruct((shard_rows, width), f32)

    widths = (head_width, head_width, head_width, hidden_width, hidden_width, hidden_width)
    made = on_chip(
        advance,
        [jax.ShapeDtypeStruct((data_count, shard_rows, slot), bf16)]
        + [rows_of(width) for width in widths]
        + [rows_of(widths[index]) for index in (0, 2, 3, 4, 5)],
        arrived_d,
        arrived_gu,
        arrived_attn,
        mom_query,
        mom_key,
        mom_value,
        mom_output,
        mom_gate,
        mom_up,
        mom_down,
        flags=my_tensor.reshape(1),
        fetch=3,
        limit=24 * 1024 * 1024,
    )
    outgoing, sum_query, part_kv, sum_output, sum_gate, sum_up, sum_down = made[:7]
    moved_query, moved_output, moved_gate, moved_up, moved_down = made[7:]

    owned = exchange(outgoing, DATA).reshape(data_count * shard_rows, slot)

    sum_half = part_kv + swap(part_kv, "tensor", 2)
    sum_other = swap(sum_half, "tensor", 1)
    sum_key = jnp.where(first_core, sum_half, sum_other)
    sum_value = jnp.where(first_core, sum_other, sum_half)
    moved_key = MUON_BETA * mom_key + sum_key
    moved_value = MUON_BETA * mom_value + sum_value
    gain_half = butterfly(gain_term, ("tensor",))
    owned, gain_half, d_input = lax.optimization_barrier((owned, gain_half, d_input))
    across = swap(owned, "tensor", 2)
    grad_gains = butterfly(gain_half, ("minor", "major"))
    across, grad_gains = lax.optimization_barrier((across, grad_gains))
    near = swap(owned, "tensor", 1)
    far = swap(across, "tensor", 1)
    turned = (my_data == owners[1]).astype(jnp.int32).reshape(1)
    ortho = newton_schulz(turned, owned, near, across, far, head_width)
    returned = exchange(ortho.reshape(data_count, shard_rows, slot), DATA)

    weights = (w_query, w_key, w_value, w_output, w_gate, w_up, w_down)
    whole_cols = [
        weights[index].shape[1] * (1 if index in (1, 2) else tensor_count) for index in range(7)
    ]
    places_of = ((0, 0), (1, 0), (1, head_width), (2, 0), (3, 0), (4, 0), (5, 0))

    def renew(back, *held):
        results = []
        for index, weight in enumerate(held):
            which, start = places_of[index]
            update = back[owners[which]][:, start : start + weight.shape[1]].astype(f32)
            factor = 0.2 * math.sqrt(max(model_width, whole_cols[index]))
            results.append(weight - MUON_RATE * (factor * update + MUON_DECAY * weight))
        return tuple(results)

    updated = on_chip(
        renew, [rows_of(weight.shape[1]) for weight in weights], returned, *weights, fetch=1,
        limit=24 * 1024 * 1024,
    )
    next_first = FIRST_DECAY * adam_first + (1.0 - FIRST_DECAY) * grad_gains
    next_second = SECOND_DECAY * adam_second + (1.0 - SECOND_DECAY) * grad_gains * grad_gains
    first_fix = 1.0 - FIRST_DECAY**STEP
    second_fix = 1.0 - SECOND_DECAY**STEP
    new_gains = gains - ADAM_RATE * (next_first / first_fix) / (
        jnp.sqrt(next_second / second_fix) + ADAM_EPSILON
    )
    return (
        block_out,
        d_input,
        sum_query,
        sum_key,
        sum_value,
        sum_output,
        sum_gate,
        sum_up,
        sum_down,
        grad_gains,
        *updated,
        moved_query,
        moved_key,
        moved_value,
        moved_output,
        moved_gate,
        moved_up,
        moved_down,
        new_gains,
        next_first,
        next_second,
    )


def solution(mesh):
    tensor_count = mesh.shape["tensor"]
    split = Mesh(
        mesh.devices.reshape(-1, 2, tensor_count), ("major", "minor", "tensor")
    )
    rows = P(("major", "minor", "tensor"), None)
    both = P(DATA, "tensor")
    data = P(DATA, None)
    matrices = (both, data, data, both, both, both, both)

    return jax.shard_map(
        body,
        mesh=split,
        in_specs=(rows, rows, data) + matrices + matrices + (P(), P(), P()),
        out_specs=(rows, rows) + matrices + (P(),) + matrices + matrices + (P(), P(), P()),
        check_vma=False,
    )
```

```python
import math

import jax
import jax.numpy as jnp
from jax import lax
from jax.experimental import pallas as pl
from jax.experimental.pallas import tpu as pltpu
from jax.sharding import Mesh
from jax.sharding import PartitionSpec as P

NS_STEPS = 5
STEP = 5


EPSILON = 1e-06
ROPE_BASE = 10000.0
MUON_BETA = 0.95
MUON_RATE = 0.04
MUON_DECAY = 0.1
POLY_FIRST = 3.4445
POLY_SECOND = -4.775
POLY_THIRD = 2.0315
FIRST_DECAY = 0.9
SECOND_DECAY = 0.95
ADAM_RATE = 0.05
ADAM_EPSILON = 1e-08
MASKED = -1e30


def rms_factor(values):
    return lax.rsqrt(jnp.mean(values * values, axis=-1, keepdims=True) + EPSILON)


def rms_norm(values, gain):
    return values * rms_factor(values) * (1.0 + gain)


def rms_pull(values, gain, cotangent):
    factor = rms_factor(values)
    scaled = cotangent * (1.0 + gain)
    inner = jnp.mean(values * scaled, axis=-1, keepdims=True)
    d_values = factor * scaled - values * (factor * factor * factor * inner)
    return d_values, cotangent * values * factor


def rotate(values, cosine, sine):
    half = values.shape[-1] // 2
    turned = jnp.concatenate([-values[..., half:], values[..., :half]], axis=-1)
    return values * cosine + turned * sine


def rotate_back(values, cosine, sine):
    half = values.shape[-1] // 2
    turned = values * sine
    turned = jnp.concatenate([turned[..., half:], -turned[..., :half]], axis=-1)
    return values * cosine + turned


def gated(gate, upper):
    return jax.nn.gelu(gate, approximate=True) * upper


def swap(values, axis, mask):
    count = lax.axis_size(axis)
    return lax.ppermute(values, axis, [(i, i ^ mask) for i in range(count)])


def dot(left, right):
    return jnp.dot(left, right, preferred_element_type=jnp.float32)


def dot_rows(left, right):
    return lax.dot_general(
        left, right, (((0,), (0,)), ((), ())), preferred_element_type=jnp.float32
    )


def dot_cols(left, right):
    return lax.dot_general(
        left, right, (((1,), (1,)), ((), ())), preferred_element_type=jnp.float32
    )


def half_sum(part):
    half = part.shape[0] // 2
    got = swap(part[half:].astype(jnp.bfloat16), "tensor", 1)
    return (part[:half] + got.astype(jnp.float32)).astype(jnp.bfloat16)


def row_sum(part):
    kept = half_sum(part)
    got = swap(kept, "tensor", 2)
    block = kept.shape[0] // 2
    got = jnp.concatenate([got[block:], got[:block]], axis=0)
    return kept.astype(jnp.float32) + got.astype(jnp.float32)


def row_sum_own(part):
    kept = half_sum(part)
    block = kept.shape[0] // 2
    got = swap(kept[block:], "tensor", 2)
    return kept[:block].astype(jnp.float32) + got.astype(jnp.float32)


def both_halves(half):
    return jnp.concatenate([half, swap(half, "tensor", 1)], axis=0)


DATA = ("major", "minor")


def exchange(values, axis):
    return lax.all_to_all(values, axis, split_axis=0, concat_axis=0, tiled=True)


def repeated(values, count):
    return jnp.broadcast_to(values[None], (count,) + values.shape)


def gather_minor(mine):
    other = swap(mine, "minor", 1)
    even = lax.axis_index("minor") == 0
    both = jnp.stack([jnp.where(even, mine, other), jnp.where(even, other, mine)], axis=1)
    return both.reshape(-1, mine.shape[-1])


def pair_sum(part):
    low = lax.axis_index("minor")
    rows = part.shape[0] // lax.axis_size(DATA)
    blocks = part.reshape(-1, 2, rows, part.shape[1])
    away = swap(lax.dynamic_index_in_dim(blocks, 1 - low, 1, keepdims=False), "minor", 1)
    here = lax.dynamic_index_in_dim(blocks, low, 1, keepdims=False)
    return (here.astype(jnp.float32) + away.astype(jnp.float32)).astype(jnp.bfloat16)


def butterfly(values, axes):
    for axis in axes:
        mask = 1
        while mask < lax.axis_size(axis):
            values = values + swap(values, axis, mask)
            mask *= 2
    return values


def total_of(blocks):
    return jnp.sum(blocks.astype(jnp.float32), axis=0)


def on_chip(math_fn, shapes, *operands, flags=None, fetch=None, limit=None):
    if shapes[0].shape[-2] % 16:
        if flags is None:
            return math_fn(*operands)
        return math_fn(flags, *operands)

    def kernel(*refs):
        scalars = () if flags is None else (refs[0],)
        ins = refs[len(scalars) : len(scalars) + len(operands)]
        outs = refs[len(scalars) + len(operands) :][: len(shapes)]
        if fetch is not None:
            held = refs[len(scalars) + len(operands) + len(shapes) : -1]
            copies = [
                pltpu.make_async_copy(ref, spot, refs[-1].at[index])
                for index, (ref, spot) in enumerate(zip(ins[fetch:], held))
            ]
            for copy in copies:
                copy.start()
            for copy in copies:
                copy.wait()
            ins = ins[:fetch] + held
        results = math_fn(*scalars, *[ref[...] for ref in ins])
        for out, result in zip(outs, results):
            out[...] = result

    specs = [pl.BlockSpec(memory_space=pltpu.VMEM)] * len(operands)
    scratch = []
    if fetch is not None:
        specs[fetch:] = [pl.BlockSpec(memory_space=pl.ANY)] * (len(operands) - fetch)
        scratch = [pltpu.VMEM(operand.shape, operand.dtype) for operand in operands[fetch:]]
        scratch.append(pltpu.SemaphoreType.DMA((len(operands) - fetch,)))
    if flags is not None:
        specs = [pl.BlockSpec(memory_space=pltpu.SMEM)] + specs
        operands_all = (flags,) + operands
    else:
        operands_all = operands
    return pl.pallas_call(
        kernel,
        out_shape=tuple(shapes),
        in_specs=specs,
        out_specs=tuple([pl.BlockSpec(memory_space=pltpu.VMEM)] * len(shapes)),
        scratch_shapes=scratch,
        compiler_params=pltpu.CompilerParams(vmem_limit_bytes=limit),
    )(*operands_all)


def diagonal_mask(size):
    rows = lax.broadcasted_iota(jnp.int32, (size, size), 0)
    return rows == lax.broadcasted_iota(jnp.int32, (size, size), 1)


def newton_schulz(flags, owned, near, across, far, pair_width):
    f32 = jnp.float32
    bf16 = jnp.bfloat16
    size, slot = owned.shape

    def kernel(flag_ref, own_ref, near_ref, across_ref, far_ref, out_ref, gram, product, both, inv):
        turned = flag_ref[0] == 1

        @pl.when(jnp.logical_not(turned))
        def _():
            total = dot_cols(own_ref[...], own_ref[...])
            for ref in (near_ref, across_ref, far_ref):
                total = total + dot_cols(ref[...], ref[...])
            norm = jnp.sum(jnp.where(diagonal_mask(size), total, 0.0))
            inverse = 1.0 / (jnp.sqrt(jnp.full((1, slot), norm, f32)) + 1e-07)
            inv[...] = inverse
            gram[...] = total * (inverse[:, :1] * inverse[:, :1])

        @pl.when(turned)
        def _():
            total = own_ref[...].astype(f32)
            for ref in (near_ref, across_ref, far_ref):
                total = total + ref[...].astype(f32)
            joined = total.astype(bf16)
            both[...] = joined
            wide = joined.astype(f32)
            squares = jnp.sum(wide * wide, axis=0, keepdims=True)
            lane = lax.broadcasted_iota(jnp.int32, (1, slot), 1)
            left = jnp.sum(jnp.where(lane < pair_width, squares, 0.0))
            right = jnp.sum(jnp.where(lane < pair_width, 0.0, squares))
            norms = jnp.where(lane < pair_width, left, right)
            inverse = 1.0 / (jnp.sqrt(norms) + 1e-07)
            inv[...] = inverse
            square = dot_rows(joined, joined)
            rows = lax.broadcasted_iota(jnp.int32, (slot, slot), 0)
            cols = lax.broadcasted_iota(jnp.int32, (slot, slot), 1)
            same = (rows < pair_width) == (cols < pair_width)
            gram[...] = jnp.zeros((size, size), f32)
            gram[:slot, :slot] = jnp.where(same, square * (inverse * inverse), 0.0)

        def step(index, carry):
            eye = diagonal_mask(size)
            square = gram[...]
            mean = jnp.sum(jnp.where(eye, square, 0.0)) / size
            shift = square - jnp.where(eye, mean, 0.0)
            level = POLY_FIRST + POLY_SECOND * mean + POLY_THIRD * mean * mean
            slope = POLY_SECOND + 2.0 * POLY_THIRD * mean
            shift16 = shift.astype(bf16)
            rest = slope * shift + POLY_THIRD * dot(shift16, shift16)
            rest16 = rest.astype(bf16)

            @pl.when(index == 0)
            def _():
                product[...] = jnp.where(eye, level, 0.0) + rest

            @pl.when(index > 0)
            def _():
                before = product[...]
                product[...] = level * before + dot(rest16, before.astype(bf16))

            @pl.when(index < NS_STEPS - 1)
            def _():
                wide = 2.0 * level * rest + dot(rest16, rest16)
                gram[...] = (
                    jnp.where(eye, level * level * mean, 0.0)
                    + level * level * shift
                    + mean * wide
                    + dot(wide.astype(bf16), shift16)
                )

            return carry

        lax.fori_loop(0, NS_STEPS, step, 0)
        narrow = product[...].astype(bf16)

        @pl.when(jnp.logical_not(turned))
        def _():
            out_ref[...] = (dot(narrow, own_ref[...]) * inv[...]).astype(bf16)

        @pl.when(turned)
        def _():
            out_ref[...] = (dot(both[...], narrow[:slot, :slot]) * inv[...]).astype(bf16)

    vmem = pl.BlockSpec(memory_space=pltpu.VMEM)
    return pl.pallas_call(
        kernel,
        out_shape=jax.ShapeDtypeStruct((size, slot), bf16),
        in_specs=[pl.BlockSpec(memory_space=pltpu.SMEM), vmem, vmem, vmem, vmem],
        out_specs=vmem,
        scratch_shapes=[
            pltpu.VMEM((size, size), f32),
            pltpu.VMEM((size, size), f32),
            pltpu.VMEM((size, slot), bf16),
            pltpu.VMEM((1, slot), f32),
        ],
        compiler_params=pltpu.CompilerParams(vmem_limit_bytes=24 * 1024 * 1024),
    )(flags, owned, near, across, far)


def body(
    block_in,
    d_output,
    doc_ids,
    w_query,
    w_key,
    w_value,
    w_output,
    w_gate,
    w_up,
    w_down,
    mom_query,
    mom_key,
    mom_value,
    mom_output,
    mom_gate,
    mom_up,
    mom_down,
    gains,
    adam_first,
    adam_second,
):
    f32 = jnp.float32
    bf16 = jnp.bfloat16
    tensor_count = lax.axis_size("tensor")
    data_count = lax.axis_size(DATA)
    major_count = lax.axis_size("major")
    my_data = lax.axis_index(DATA)
    my_tensor = lax.axis_index("tensor")
    own = block_in.shape[0]
    model_width = block_in.shape[1]
    head_width = w_key.shape[1]
    hidden_width = w_gate.shape[1]
    seq_len = doc_ids.shape[1]
    shard_rows = w_key.shape[0]
    assert tensor_count == 4 and doc_ids.shape[0] == 1 and w_query.shape[1] == head_width
    assert own * tensor_count == seq_len and hidden_width == 2 * head_width
    scale = head_width ** (-0.5)
    pre_attn = gains[0:model_width]
    post_attn = gains[model_width : 2 * model_width]
    pre_ffn = gains[2 * model_width : 3 * model_width]
    post_ffn = gains[3 * model_width : 4 * model_width]
    gain_q = gains[4 * model_width : 4 * model_width + head_width]
    gain_k = gains[4 * model_width + head_width :]
    first_core = (my_tensor & 1) == 0

    order = (0, 2, 1, 3)

    def pack(flags, query, key, value, output, gate, upper, down):
        half = jnp.where(flags[0] == 0, key, value)
        attn = jnp.concatenate([query, half, output], axis=1).astype(bf16)
        gate_up = jnp.concatenate([gate, upper], axis=1).astype(bf16)
        return (
            repeated(attn, major_count),
            repeated(gate_up, major_count),
            down.astype(bf16),
        )

    packed_attn, packed_gu, packed_d = on_chip(
        pack,
        [
            jax.ShapeDtypeStruct((major_count, shard_rows, 3 * head_width), bf16),
            jax.ShapeDtypeStruct((major_count, shard_rows, 2 * hidden_width), bf16),
            jax.ShapeDtypeStruct((shard_rows, hidden_width), bf16),
        ],
        w_query,
        w_key,
        w_value,
        w_output,
        w_gate,
        w_up,
        w_down,
        flags=(my_tensor & 1).reshape(1),
        fetch=0,
    )
    major_attn = exchange(packed_attn, "major")
    packed_gu, major_attn = lax.optimization_barrier((packed_gu, major_attn))
    weights_attn = gather_minor(major_attn)
    major_gu = exchange(packed_gu, "major")
    other_d = swap(packed_d, "minor", 1)
    even = lax.axis_index("minor") == 0
    pair_rows = jnp.concatenate(
        [jnp.where(even, packed_d, other_d), jnp.where(even, other_d, packed_d)], axis=0
    )
    pair_rows, major_gu = lax.optimization_barrier((repeated(pair_rows, major_count), major_gu))
    weights_gu = gather_minor(major_gu)
    weight_d = exchange(pair_rows, "major").reshape(model_width, hidden_width)
    weight_q = weights_attn[:, :head_width]
    weight_half = weights_attn[:, head_width : 2 * head_width]
    weight_o = weights_attn[:, 2 * head_width :]
    weight_other = swap(weight_half, "tensor", 1)
    weights_qkv = jnp.concatenate(
        [
            weight_q,
            jnp.where(first_core, weight_half, weight_other),
            jnp.where(first_core, weight_other, weight_half),
        ],
        axis=1,
    )

    other_in = swap(block_in, "tensor", 2)
    rows_in = jnp.concatenate([block_in, other_in], axis=0)
    normed_half = rms_norm(rows_in, pre_attn).astype(bf16)
    other_half = swap(normed_half, "tensor", 1)
    normed_one = jnp.concatenate([normed_half, other_half], axis=0)
    cot_rows = jnp.concatenate([d_output, swap(d_output, "tensor", 2)], axis=0)
    normed_one, cot_rows = lax.optimization_barrier((normed_one, cot_rows))

    doc_blocks = doc_ids.reshape(tensor_count, own)
    docs = jnp.concatenate(
        [lax.dynamic_index_in_dim(doc_blocks, my_tensor ^ j, 0, keepdims=False) for j in order]
    )
    places = jnp.concatenate(
        [(my_tensor ^ j) * own + jnp.arange(own, dtype=jnp.int32) for j in order]
    )
    first = jnp.sum((docs[None, :] < docs[:, None]).astype(jnp.int32), axis=-1)
    offset = (places - first).astype(f32)
    freqs = ROPE_BASE ** (-(2.0 * jnp.arange(head_width // 2, dtype=f32)) / head_width)
    angles = offset[:, None] * freqs
    cosine, sine = jnp.cos(angles), jnp.sin(angles)
    cosine = jnp.concatenate([cosine, cosine], axis=-1)
    sine = jnp.concatenate([sine, sine], axis=-1)
    allowed = (docs[None, :] == docs[:, None]) & (places[None, :] <= places[:, None])

    raw = dot(normed_one, weights_qkv)
    queries = raw[:, :head_width]
    keys = raw[:, head_width : 2 * head_width]
    values = raw[:, 2 * head_width :].astype(bf16)
    query_rot = rotate(rms_norm(queries, gain_q), cosine, sine).astype(bf16)
    key_rot = rotate(rms_norm(keys, gain_k), cosine, sine).astype(bf16)
    scores = jnp.where(allowed, dot_cols(query_rot, key_rot) * scale, MASKED)
    top = jnp.max(scores, axis=-1, keepdims=True)
    log_total = top + jnp.log(jnp.sum(jnp.exp(scores - top), axis=-1, keepdims=True))
    prob_full = jnp.exp(scores - log_total)
    probs = prob_full.astype(bf16)
    heads = dot(probs, values).astype(bf16)

    attn = row_sum(dot_cols(heads, weight_o))
    middle = rows_in + rms_norm(attn, post_attn)
    normed_two = both_halves(rms_norm(middle, pre_ffn).astype(bf16))
    gate_up = dot(normed_two, weights_gu)
    gate = gate_up[:, :hidden_width]
    upper = gate_up[:, hidden_width:]
    hidden = gated(gate, upper).astype(bf16)
    branch = row_sum(dot_cols(hidden, weight_d))
    block_out = middle[:own] + rms_norm(branch[:own], post_ffn)

    d_branch, g_post_ffn = rms_pull(branch, post_ffn, cot_rows)
    branch_low = both_halves(d_branch.astype(bf16))
    grad_d = dot_rows(branch_low, hidden).astype(bf16)
    arrived_d = exchange(grad_d.reshape(major_count, -1, hidden_width), "major")
    d_hidden = dot(branch_low, weight_d)
    d_gate, d_upper = jax.vjp(gated, gate, upper)[1](d_hidden)
    gu_low = jnp.concatenate([d_gate.astype(bf16), d_upper.astype(bf16)], axis=1)
    pair_gu = pair_sum(dot_rows(normed_two, gu_low).astype(bf16))
    pair_gu, arrived_d = lax.optimization_barrier((pair_gu, arrived_d))
    both_d = total_of(arrived_d).reshape(2, shard_rows, hidden_width)
    low = lax.axis_index("minor")
    away_d = lax.dynamic_index_in_dim(both_d, 1 - low, 0, keepdims=False).astype(bf16)
    away_d = swap(away_d, "minor", 1)
    total_d = lax.dynamic_index_in_dim(both_d, low, 0, keepdims=False) + away_d.astype(f32)
    arrived_gu = exchange(pair_gu, "major")
    d_normed_two = row_sum(dot_cols(gu_low, weights_gu))
    d_mid_extra, g_pre_ffn = rms_pull(middle, pre_ffn, d_normed_two)
    d_middle = cot_rows + d_mid_extra
    d_attn, g_post_attn = rms_pull(attn, post_attn, d_middle)
    attn_low = both_halves(d_attn.astype(bf16))
    grad_o = dot_rows(attn_low, heads).astype(bf16)

    d_heads = dot(attn_low, weight_o).astype(bf16)
    delta = jnp.sum(d_heads.astype(f32) * heads.astype(f32), axis=-1, keepdims=True)
    d_probs = dot_cols(d_heads, values)
    d_scores = (prob_full * (d_probs - delta) * scale).astype(bf16)
    d_qrot = dot(d_scores, key_rot)
    d_krot = dot_rows(d_scores, query_rot)
    d_vals = dot_rows(probs, d_heads)
    d_queries, g_query = rms_pull(queries, gain_q, rotate_back(d_qrot, cosine, sine))
    d_keys, g_key = rms_pull(keys, gain_k, rotate_back(d_krot, cosine, sine))
    qkv_low = jnp.concatenate(
        [d_queries.astype(bf16), d_keys.astype(bf16), d_vals.astype(bf16)], axis=1
    )
    grad_kv = dot_rows(normed_one, qkv_low[:, head_width:])
    grad_key, grad_value = grad_kv[:, :head_width], grad_kv[:, head_width:]
    got = swap(jnp.where(first_core, grad_value, grad_key).astype(bf16), "tensor", 1)
    grad_half = jnp.where(first_core, grad_key, grad_value) + got.astype(f32)
    grad_query = dot_rows(normed_one, qkv_low[:, :head_width])
    grad_attn = jnp.concatenate(
        [grad_query.astype(bf16), grad_half.astype(bf16), grad_o], axis=1
    )
    grad_attn, arrived_gu = lax.optimization_barrier((grad_attn, arrived_gu))
    arrived_attn = exchange(grad_attn.reshape(data_count, shard_rows, -1), DATA)

    d_normed_one = row_sum_own(dot_cols(qkv_low, weights_qkv))
    d_in_extra, g_pre_attn = rms_pull(block_in, pre_attn, d_normed_one)
    d_input = d_middle[:own] + d_in_extra
    gain_term = jnp.concatenate(
        [
            jnp.sum(g_pre_attn, axis=0),
            jnp.sum(g_post_attn[:own], axis=0),
            jnp.sum(g_pre_ffn[:own], axis=0),
            jnp.sum(g_post_ffn[:own], axis=0),
            jnp.sum(g_query, axis=0),
            jnp.sum(g_key, axis=0),
        ]
    )

    slot = hidden_width
    owners = [index * data_count // 6 for index in range(6)]

    def advance(flags, whole_d, moved_gu, moved_attn, *moments):
        m_query, m_key, m_value, m_output, m_gate, m_up, m_down = moments
        low = total_of(moved_attn)
        wide = total_of(moved_gu)
        terms = (
            low[:, :head_width],
            low[:, head_width : 2 * head_width],
            low[:, 2 * head_width :],
            wide[:, :hidden_width],
            wide[:, hidden_width:],
            whole_d,
        )
        share = jnp.where(flags[0] < 2, 1.0, 0.0)
        even = flags[0] % 2 == 0
        held = (
            m_query,
            jnp.where(even, m_key, m_value) * share,
            m_output,
            m_gate,
            m_up,
            m_down,
        )
        moved = [MUON_BETA * moment + term for moment, term in zip(held, terms)]
        blocks = []
        for index in range(data_count):
            if index not in owners:
                blocks.append(jnp.zeros((shard_rows, slot), bf16))
                continue
            which = owners.index(index)
            push = (terms[which] + MUON_BETA * moved[which]).astype(bf16)
            if which == 1:
                none = jnp.zeros_like(push)
                push = jnp.concatenate(
                    [jnp.where(even, push, none), jnp.where(even, none, push)], axis=1
                )
            if push.shape[1] < slot:
                empty = jnp.zeros((shard_rows, slot - push.shape[1]), bf16)
                push = jnp.concatenate([push, empty], axis=1)
            blocks.append(push)
        keep = (0, 2, 3, 4, 5)
        return (
            (jnp.stack(blocks),)
            + tuple(terms)
            + tuple(moved[index] for index in keep)
        )

    def rows_of(width):
        return jax.ShapeDtypeStruct((shard_rows, width), f32)

    widths = (head_width, head_width, head_width, hidden_width, hidden_width, hidden_width)
    made = on_chip(
        advance,
        [jax.ShapeDtypeStruct((data_count, shard_rows, slot), bf16)]
        + [rows_of(width) for width in widths]
        + [rows_of(widths[index]) for index in (0, 2, 3, 4, 5)],
        total_d,
        arrived_gu,
        arrived_attn,
        mom_query,
        mom_key,
        mom_value,
        mom_output,
        mom_gate,
        mom_up,
        mom_down,
        flags=my_tensor.reshape(1),
        fetch=3,
        limit=24 * 1024 * 1024,
    )
    outgoing, sum_query, part_kv, sum_output, sum_gate, sum_up, sum_down = made[:7]
    moved_query, moved_output, moved_gate, moved_up, moved_down = made[7:]

    owned = exchange(outgoing, DATA).reshape(data_count * shard_rows, slot)

    sum_half = part_kv + swap(part_kv, "tensor", 2)
    sum_other = swap(sum_half, "tensor", 1)
    sum_key = jnp.where(first_core, sum_half, sum_other)
    sum_value = jnp.where(first_core, sum_other, sum_half)
    moved_key = MUON_BETA * mom_key + sum_key
    moved_value = MUON_BETA * mom_value + sum_value
    gain_half = butterfly(gain_term, ("tensor",))
    owned, gain_half, d_input = lax.optimization_barrier((owned, gain_half, d_input))
    across = swap(owned, "tensor", 2)
    grad_gains = butterfly(gain_half, ("minor", "major"))
    across, grad_gains = lax.optimization_barrier((across, grad_gains))
    near = swap(owned, "tensor", 1)
    far = swap(across, "tensor", 1)
    turned = (my_data == owners[1]).astype(jnp.int32).reshape(1)
    ortho = newton_schulz(turned, owned, near, across, far, head_width)
    returned = exchange(ortho.reshape(data_count, shard_rows, slot), DATA)

    weights = (w_query, w_key, w_value, w_output, w_gate, w_up, w_down)
    whole_cols = [
        weights[index].shape[1] * (1 if index in (1, 2) else tensor_count) for index in range(7)
    ]
    places_of = ((0, 0), (1, 0), (1, head_width), (2, 0), (3, 0), (4, 0), (5, 0))

    def renew(back, *held):
        results = []
        for index, weight in enumerate(held):
            which, start = places_of[index]
            update = back[owners[which]][:, start : start + weight.shape[1]].astype(f32)
            factor = 0.2 * math.sqrt(max(model_width, whole_cols[index]))
            results.append(weight - MUON_RATE * (factor * update + MUON_DECAY * weight))
        return tuple(results)

    updated = on_chip(
        renew, [rows_of(weight.shape[1]) for weight in weights], returned, *weights, fetch=1,
        limit=24 * 1024 * 1024,
    )
    next_first = FIRST_DECAY * adam_first + (1.0 - FIRST_DECAY) * grad_gains
    next_second = SECOND_DECAY * adam_second + (1.0 - SECOND_DECAY) * grad_gains * grad_gains
    first_fix = 1.0 - FIRST_DECAY**STEP
    second_fix = 1.0 - SECOND_DECAY**STEP
    new_gains = gains - ADAM_RATE * (next_first / first_fix) / (
        jnp.sqrt(next_second / second_fix) + ADAM_EPSILON
    )
    return (
        block_out,
        d_input,
        sum_query,
        sum_key,
        sum_value,
        sum_output,
        sum_gate,
        sum_up,
        sum_down,
        grad_gains,
        *updated,
        moved_query,
        moved_key,
        moved_value,
        moved_output,
        moved_gate,
        moved_up,
        moved_down,
        new_gains,
        next_first,
        next_second,
    )


def solution(mesh):
    tensor_count = mesh.shape["tensor"]
    split = Mesh(
        mesh.devices.reshape(-1, 2, tensor_count), ("major", "minor", "tensor")
    )
    rows = P(("major", "minor", "tensor"), None)
    both = P(DATA, "tensor")
    data = P(DATA, None)
    matrices = (both, data, data, both, both, both, both)

    return jax.shard_map(
        body,
        mesh=split,
        in_specs=(rows, rows, data) + matrices + matrices + (P(), P(), P()),
        out_specs=(rows, rows) + matrices + (P(),) + matrices + matrices + (P(), P(), P()),
        check_vma=False,
    )
```

```python
import math

import jax
import jax.numpy as jnp
from jax import lax
from jax.experimental import pallas as pl
from jax.experimental.pallas import tpu as pltpu
from jax.sharding import Mesh
from jax.sharding import PartitionSpec as P

NS_STEPS = 5
STEP = 5


EPSILON = 1e-06
ROPE_BASE = 10000.0
MUON_BETA = 0.95
MUON_RATE = 0.04
MUON_DECAY = 0.1
POLY_FIRST = 3.4445
POLY_SECOND = -4.775
POLY_THIRD = 2.0315
FIRST_DECAY = 0.9
SECOND_DECAY = 0.95
ADAM_RATE = 0.05
ADAM_EPSILON = 1e-08
MASKED = -1e30


def rms_factor(values):
    return lax.rsqrt(jnp.mean(values * values, axis=-1, keepdims=True) + EPSILON)


def rms_norm(values, gain):
    return values * rms_factor(values) * (1.0 + gain)


def rms_pull(values, gain, cotangent):
    factor = rms_factor(values)
    scaled = cotangent * (1.0 + gain)
    inner = jnp.mean(values * scaled, axis=-1, keepdims=True)
    d_values = factor * scaled - values * (factor * factor * factor * inner)
    return d_values, cotangent * values * factor


def rotate(values, cosine, sine):
    half = values.shape[-1] // 2
    turned = jnp.concatenate([-values[..., half:], values[..., :half]], axis=-1)
    return values * cosine + turned * sine


def rotate_back(values, cosine, sine):
    half = values.shape[-1] // 2
    turned = values * sine
    turned = jnp.concatenate([turned[..., half:], -turned[..., :half]], axis=-1)
    return values * cosine + turned


def gated(gate, upper):
    return jax.nn.gelu(gate, approximate=True) * upper


def swap(values, axis, mask):
    count = lax.axis_size(axis)
    return lax.ppermute(values, axis, [(i, i ^ mask) for i in range(count)])


def dot(left, right):
    return jnp.dot(left, right, preferred_element_type=jnp.float32)


def dot_rows(left, right):
    return lax.dot_general(
        left, right, (((0,), (0,)), ((), ())), preferred_element_type=jnp.float32
    )


def dot_cols(left, right):
    return lax.dot_general(
        left, right, (((1,), (1,)), ((), ())), preferred_element_type=jnp.float32
    )


def half_sum(part):
    half = part.shape[0] // 2
    got = swap(part[half:].astype(jnp.bfloat16), "tensor", 1)
    return (part[:half] + got.astype(jnp.float32)).astype(jnp.bfloat16)


def row_sum(part):
    kept = half_sum(part)
    got = swap(kept, "tensor", 2)
    block = kept.shape[0] // 2
    got = jnp.concatenate([got[block:], got[:block]], axis=0)
    return kept.astype(jnp.float32) + got.astype(jnp.float32)


def row_sum_own(part):
    kept = half_sum(part)
    block = kept.shape[0] // 2
    got = swap(kept[block:], "tensor", 2)
    return kept[:block].astype(jnp.float32) + got.astype(jnp.float32)


def both_halves(half):
    return jnp.concatenate([half, swap(half, "tensor", 1)], axis=0)


DATA = ("major", "minor")


def exchange(values, axis):
    return lax.all_to_all(values, axis, split_axis=0, concat_axis=0, tiled=True)


def repeated(values, count):
    return jnp.broadcast_to(values[None], (count,) + values.shape)


def gather_minor(mine):
    other = swap(mine, "minor", 1)
    even = lax.axis_index("minor") == 0
    both = jnp.stack([jnp.where(even, mine, other), jnp.where(even, other, mine)], axis=1)
    return both.reshape(-1, mine.shape[-1])


def pair_sum(part):
    low = lax.axis_index("minor")
    rows = part.shape[0] // lax.axis_size(DATA)
    blocks = part.reshape(-1, 2, rows, part.shape[1])
    away = swap(lax.dynamic_index_in_dim(blocks, 1 - low, 1, keepdims=False), "minor", 1)
    here = lax.dynamic_index_in_dim(blocks, low, 1, keepdims=False)
    return (here.astype(jnp.float32) + away.astype(jnp.float32)).astype(jnp.bfloat16)


def butterfly(values, axes):
    for axis in axes:
        mask = 1
        while mask < lax.axis_size(axis):
            values = values + swap(values, axis, mask)
            mask *= 2
    return values


def total_of(blocks):
    return jnp.sum(blocks.astype(jnp.float32), axis=0)


def on_chip(math_fn, shapes, *operands, flags=None, fetch=None, limit=None):
    if shapes[0].shape[-2] % 16:
        if flags is None:
            return math_fn(*operands)
        return math_fn(flags, *operands)

    def kernel(*refs):
        scalars = () if flags is None else (refs[0],)
        ins = refs[len(scalars) : len(scalars) + len(operands)]
        outs = refs[len(scalars) + len(operands) :][: len(shapes)]
        if fetch is not None:
            held = refs[len(scalars) + len(operands) + len(shapes) : -1]
            copies = [
                pltpu.make_async_copy(ref, spot, refs[-1].at[index])
                for index, (ref, spot) in enumerate(zip(ins[fetch:], held))
            ]
            for copy in copies:
                copy.start()
            for copy in copies:
                copy.wait()
            ins = ins[:fetch] + held
        results = math_fn(*scalars, *[ref[...] for ref in ins])
        for out, result in zip(outs, results):
            out[...] = result

    specs = [pl.BlockSpec(memory_space=pltpu.VMEM)] * len(operands)
    scratch = []
    if fetch is not None:
        specs[fetch:] = [pl.BlockSpec(memory_space=pl.ANY)] * (len(operands) - fetch)
        scratch = [pltpu.VMEM(operand.shape, operand.dtype) for operand in operands[fetch:]]
        scratch.append(pltpu.SemaphoreType.DMA((len(operands) - fetch,)))
    if flags is not None:
        specs = [pl.BlockSpec(memory_space=pltpu.SMEM)] + specs
        operands_all = (flags,) + operands
    else:
        operands_all = operands
    return pl.pallas_call(
        kernel,
        out_shape=tuple(shapes),
        in_specs=specs,
        out_specs=tuple([pl.BlockSpec(memory_space=pltpu.VMEM)] * len(shapes)),
        scratch_shapes=scratch,
        compiler_params=pltpu.CompilerParams(vmem_limit_bytes=limit),
    )(*operands_all)


def diagonal_mask(size):
    rows = lax.broadcasted_iota(jnp.int32, (size, size), 0)
    return rows == lax.broadcasted_iota(jnp.int32, (size, size), 1)


def newton_schulz(flags, owned, near, across, far, pair_width):
    f32 = jnp.float32
    bf16 = jnp.bfloat16
    size, slot = owned.shape

    def kernel(flag_ref, own_ref, near_ref, across_ref, far_ref, out_ref, gram, product, both, inv):
        turned = flag_ref[0] == 1

        @pl.when(jnp.logical_not(turned))
        def _():
            total = dot_cols(own_ref[...], own_ref[...])
            for ref in (near_ref, across_ref, far_ref):
                total = total + dot_cols(ref[...], ref[...])
            norm = jnp.sum(jnp.where(diagonal_mask(size), total, 0.0))
            inverse = 1.0 / (jnp.sqrt(jnp.full((1, slot), norm, f32)) + 1e-07)
            inv[...] = inverse
            gram[...] = total * (inverse[:, :1] * inverse[:, :1])

        @pl.when(turned)
        def _():
            total = own_ref[...].astype(f32)
            for ref in (near_ref, across_ref, far_ref):
                total = total + ref[...].astype(f32)
            joined = total.astype(bf16)
            both[...] = joined
            wide = joined.astype(f32)
            squares = jnp.sum(wide * wide, axis=0, keepdims=True)
            lane = lax.broadcasted_iota(jnp.int32, (1, slot), 1)
            left = jnp.sum(jnp.where(lane < pair_width, squares, 0.0))
            right = jnp.sum(jnp.where(lane < pair_width, 0.0, squares))
            norms = jnp.where(lane < pair_width, left, right)
            inverse = 1.0 / (jnp.sqrt(norms) + 1e-07)
            inv[...] = inverse
            square = dot_rows(joined, joined)
            rows = lax.broadcasted_iota(jnp.int32, (slot, slot), 0)
            cols = lax.broadcasted_iota(jnp.int32, (slot, slot), 1)
            same = (rows < pair_width) == (cols < pair_width)
            gram[...] = jnp.zeros((size, size), f32)
            gram[:slot, :slot] = jnp.where(same, square * (inverse * inverse), 0.0)

        def step(index, carry):
            eye = diagonal_mask(size)
            square = gram[...]
            mean = jnp.sum(jnp.where(eye, square, 0.0)) / size
            shift = square - jnp.where(eye, mean, 0.0)
            level = POLY_FIRST + POLY_SECOND * mean + POLY_THIRD * mean * mean
            slope = POLY_SECOND + 2.0 * POLY_THIRD * mean
            shift16 = shift.astype(bf16)
            rest = slope * shift + POLY_THIRD * dot(shift16, shift16)
            rest16 = rest.astype(bf16)

            def advance(square_rest):
                wide = 2.0 * level * rest + square_rest
                gram[...] = (
                    jnp.where(eye, level * level * mean, 0.0)
                    + level * level * shift
                    + mean * wide
                    + dot(wide.astype(bf16), shift16)
                )

            @pl.when(index == 0)
            def _():
                product[...] = jnp.where(eye, level, 0.0) + rest
                advance(dot(rest16, rest16))

            @pl.when((index > 0) & (index < NS_STEPS - 1))
            def _():
                before = product[...]
                pair = jnp.concatenate([before.astype(bf16), rest16], axis=1)
                made = dot(rest16, pair)
                product[...] = level * before + made[:, :size]
                advance(made[:, size:])

            @pl.when(index == NS_STEPS - 1)
            def _():
                before = product[...]
                product[...] = level * before + dot(rest16, before.astype(bf16))

            return carry

        lax.fori_loop(0, NS_STEPS, step, 0)
        narrow = product[...].astype(bf16)

        @pl.when(jnp.logical_not(turned))
        def _():
            out_ref[...] = (dot(narrow, own_ref[...]) * inv[...]).astype(bf16)

        @pl.when(turned)
        def _():
            out_ref[...] = (dot(both[...], narrow[:slot, :slot]) * inv[...]).astype(bf16)

    vmem = pl.BlockSpec(memory_space=pltpu.VMEM)
    return pl.pallas_call(
        kernel,
        out_shape=jax.ShapeDtypeStruct((size, slot), bf16),
        in_specs=[pl.BlockSpec(memory_space=pltpu.SMEM), vmem, vmem, vmem, vmem],
        out_specs=vmem,
        scratch_shapes=[
            pltpu.VMEM((size, size), f32),
            pltpu.VMEM((size, size), f32),
            pltpu.VMEM((size, slot), bf16),
            pltpu.VMEM((1, slot), f32),
        ],
        compiler_params=pltpu.CompilerParams(vmem_limit_bytes=24 * 1024 * 1024),
    )(flags, owned, near, across, far)


def body(
    block_in,
    d_output,
    doc_ids,
    w_query,
    w_key,
    w_value,
    w_output,
    w_gate,
    w_up,
    w_down,
    mom_query,
    mom_key,
    mom_value,
    mom_output,
    mom_gate,
    mom_up,
    mom_down,
    gains,
    adam_first,
    adam_second,
):
    f32 = jnp.float32
    bf16 = jnp.bfloat16
    tensor_count = lax.axis_size("tensor")
    data_count = lax.axis_size(DATA)
    major_count = lax.axis_size("major")
    my_data = lax.axis_index(DATA)
    my_tensor = lax.axis_index("tensor")
    own = block_in.shape[0]
    model_width = block_in.shape[1]
    head_width = w_key.shape[1]
    hidden_width = w_gate.shape[1]
    seq_len = doc_ids.shape[1]
    shard_rows = w_key.shape[0]
    assert tensor_count == 4 and doc_ids.shape[0] == 1 and w_query.shape[1] == head_width
    assert own * tensor_count == seq_len and hidden_width == 2 * head_width
    scale = head_width ** (-0.5)
    pre_attn = gains[0:model_width]
    post_attn = gains[model_width : 2 * model_width]
    pre_ffn = gains[2 * model_width : 3 * model_width]
    post_ffn = gains[3 * model_width : 4 * model_width]
    gain_q = gains[4 * model_width : 4 * model_width + head_width]
    gain_k = gains[4 * model_width + head_width :]
    first_core = (my_tensor & 1) == 0

    order = (0, 2, 1, 3)

    def pack(flags, query, key, value, output, gate, upper, down):
        half = jnp.where(flags[0] == 0, key, value)
        attn = jnp.concatenate([query, half, output], axis=1).astype(bf16)
        gate_up = jnp.concatenate([gate, upper], axis=1).astype(bf16)
        return (
            repeated(attn, major_count),
            repeated(gate_up, major_count),
            down.astype(bf16),
        )

    packed_attn, packed_gu, packed_d = on_chip(
        pack,
        [
            jax.ShapeDtypeStruct((major_count, shard_rows, 3 * head_width), bf16),
            jax.ShapeDtypeStruct((major_count, shard_rows, 2 * hidden_width), bf16),
            jax.ShapeDtypeStruct((shard_rows, hidden_width), bf16),
        ],
        w_query,
        w_key,
        w_value,
        w_output,
        w_gate,
        w_up,
        w_down,
        flags=(my_tensor & 1).reshape(1),
        fetch=0,
    )
    major_attn = exchange(packed_attn, "major")
    packed_gu, major_attn = lax.optimization_barrier((packed_gu, major_attn))
    weights_attn = gather_minor(major_attn)
    major_gu = exchange(packed_gu, "major")
    other_d = swap(packed_d, "minor", 1)
    even = lax.axis_index("minor") == 0
    pair_rows = jnp.concatenate(
        [jnp.where(even, packed_d, other_d), jnp.where(even, other_d, packed_d)], axis=0
    )
    pair_rows, major_gu = lax.optimization_barrier((repeated(pair_rows, major_count), major_gu))
    weights_gu = gather_minor(major_gu)
    weight_d = exchange(pair_rows, "major").reshape(model_width, hidden_width)
    weight_q = weights_attn[:, :head_width]
    weight_half = weights_attn[:, head_width : 2 * head_width]
    weight_o = weights_attn[:, 2 * head_width :]
    weight_other = swap(weight_half, "tensor", 1)
    weights_qkv = jnp.concatenate(
        [
            weight_q,
            jnp.where(first_core, weight_half, weight_other),
            jnp.where(first_core, weight_other, weight_half),
        ],
        axis=1,
    )

    other_in = swap(block_in, "tensor", 2)
    rows_in = jnp.concatenate([block_in, other_in], axis=0)
    normed_half = rms_norm(rows_in, pre_attn).astype(bf16)
    other_half = swap(normed_half, "tensor", 1)
    normed_one = jnp.concatenate([normed_half, other_half], axis=0)
    cot_rows = jnp.concatenate([d_output, swap(d_output, "tensor", 2)], axis=0)
    normed_one, cot_rows = lax.optimization_barrier((normed_one, cot_rows))

    doc_blocks = doc_ids.reshape(tensor_count, own)
    docs = jnp.concatenate(
        [lax.dynamic_index_in_dim(doc_blocks, my_tensor ^ j, 0, keepdims=False) for j in order]
    )
    places = jnp.concatenate(
        [(my_tensor ^ j) * own + jnp.arange(own, dtype=jnp.int32) for j in order]
    )
    first = jnp.sum((docs[None, :] < docs[:, None]).astype(jnp.int32), axis=-1)
    offset = (places - first).astype(f32)
    freqs = ROPE_BASE ** (-(2.0 * jnp.arange(head_width // 2, dtype=f32)) / head_width)
    angles = offset[:, None] * freqs
    cosine, sine = jnp.cos(angles), jnp.sin(angles)
    cosine = jnp.concatenate([cosine, cosine], axis=-1)
    sine = jnp.concatenate([sine, sine], axis=-1)
    allowed = (docs[None, :] == docs[:, None]) & (places[None, :] <= places[:, None])

    raw = dot(normed_one, weights_qkv)
    queries = raw[:, :head_width]
    keys = raw[:, head_width : 2 * head_width]
    values = raw[:, 2 * head_width :].astype(bf16)
    query_rot = rotate(rms_norm(queries, gain_q), cosine, sine).astype(bf16)
    key_rot = rotate(rms_norm(keys, gain_k), cosine, sine).astype(bf16)
    scores = jnp.where(allowed, dot_cols(query_rot, key_rot) * scale, MASKED)
    top = jnp.max(scores, axis=-1, keepdims=True)
    log_total = top + jnp.log(jnp.sum(jnp.exp(scores - top), axis=-1, keepdims=True))
    prob_full = jnp.exp(scores - log_total)
    probs = prob_full.astype(bf16)
    heads = dot(probs, values).astype(bf16)

    attn = row_sum(dot_cols(heads, weight_o))
    middle = rows_in + rms_norm(attn, post_attn)
    normed_two = both_halves(rms_norm(middle, pre_ffn).astype(bf16))
    gate_up = dot(normed_two, weights_gu)
    gate = gate_up[:, :hidden_width]
    upper = gate_up[:, hidden_width:]
    hidden = gated(gate, upper).astype(bf16)
    branch = row_sum(dot_cols(hidden, weight_d))
    block_out = middle[:own] + rms_norm(branch[:own], post_ffn)

    d_branch, g_post_ffn = rms_pull(branch, post_ffn, cot_rows)
    branch_low = both_halves(d_branch.astype(bf16))
    grad_d = dot_rows(branch_low, hidden).astype(bf16)
    arrived_d = exchange(grad_d.reshape(major_count, -1, hidden_width), "major")
    d_hidden = dot(branch_low, weight_d)
    d_gate, d_upper = jax.vjp(gated, gate, upper)[1](d_hidden)
    gu_low = jnp.concatenate([d_gate.astype(bf16), d_upper.astype(bf16)], axis=1)
    pair_gu = pair_sum(dot_rows(normed_two, gu_low).astype(bf16))
    pair_gu, arrived_d = lax.optimization_barrier((pair_gu, arrived_d))
    both_d = total_of(arrived_d).reshape(2, shard_rows, hidden_width)
    low = lax.axis_index("minor")
    away_d = lax.dynamic_index_in_dim(both_d, 1 - low, 0, keepdims=False).astype(bf16)
    away_d = swap(away_d, "minor", 1)
    total_d = lax.dynamic_index_in_dim(both_d, low, 0, keepdims=False) + away_d.astype(f32)
    arrived_gu = exchange(pair_gu, "major")
    d_normed_two = row_sum(dot_cols(gu_low, weights_gu))
    d_mid_extra, g_pre_ffn = rms_pull(middle, pre_ffn, d_normed_two)
    d_middle = cot_rows + d_mid_extra
    d_attn, g_post_attn = rms_pull(attn, post_attn, d_middle)
    attn_low = both_halves(d_attn.astype(bf16))
    grad_o = dot_rows(attn_low, heads).astype(bf16)

    d_heads = dot(attn_low, weight_o).astype(bf16)
    delta = jnp.sum(d_heads.astype(f32) * heads.astype(f32), axis=-1, keepdims=True)
    d_probs = dot_cols(d_heads, values)
    d_scores = (prob_full * (d_probs - delta) * scale).astype(bf16)
    d_qrot = dot(d_scores, key_rot)
    d_krot = dot_rows(d_scores, query_rot)
    d_vals = dot_rows(probs, d_heads)
    d_queries, g_query = rms_pull(queries, gain_q, rotate_back(d_qrot, cosine, sine))
    d_keys, g_key = rms_pull(keys, gain_k, rotate_back(d_krot, cosine, sine))
    qkv_low = jnp.concatenate(
        [d_queries.astype(bf16), d_keys.astype(bf16), d_vals.astype(bf16)], axis=1
    )
    grad_kv = dot_rows(normed_one, qkv_low[:, head_width:])
    grad_key, grad_value = grad_kv[:, :head_width], grad_kv[:, head_width:]
    got = swap(jnp.where(first_core, grad_value, grad_key).astype(bf16), "tensor", 1)
    grad_half = jnp.where(first_core, grad_key, grad_value) + got.astype(f32)
    grad_query = dot_rows(normed_one, qkv_low[:, :head_width])
    grad_o, arrived_gu = lax.optimization_barrier((grad_o, arrived_gu))
    grad_attn = jnp.concatenate(
        [grad_query.astype(bf16), grad_half.astype(bf16), grad_o], axis=1
    )
    arrived_attn = exchange(grad_attn.reshape(data_count, shard_rows, -1), DATA)

    d_normed_one = row_sum_own(dot_cols(qkv_low, weights_qkv))
    d_in_extra, g_pre_attn = rms_pull(block_in, pre_attn, d_normed_one)
    d_input = d_middle[:own] + d_in_extra
    gain_term = jnp.concatenate(
        [
            jnp.sum(g_pre_attn, axis=0),
            jnp.sum(g_post_attn[:own], axis=0),
            jnp.sum(g_pre_ffn[:own], axis=0),
            jnp.sum(g_post_ffn[:own], axis=0),
            jnp.sum(g_query, axis=0),
            jnp.sum(g_key, axis=0),
        ]
    )

    slot = hidden_width
    owners = [index * data_count // 6 for index in range(6)]

    def advance(flags, whole_d, moved_gu, moved_attn, *moments):
        m_query, m_key, m_value, m_output, m_gate, m_up, m_down = moments
        low = total_of(moved_attn)
        wide = total_of(moved_gu)
        terms = (
            low[:, :head_width],
            low[:, head_width : 2 * head_width],
            low[:, 2 * head_width :],
            wide[:, :hidden_width],
            wide[:, hidden_width:],
            whole_d,
        )
        share = jnp.where(flags[0] < 2, 1.0, 0.0)
        even = flags[0] % 2 == 0
        held = (
            m_query,
            jnp.where(even, m_key, m_value) * share,
            m_output,
            m_gate,
            m_up,
            m_down,
        )
        moved = [MUON_BETA * moment + term for moment, term in zip(held, terms)]
        blocks = []
        for index in range(data_count):
            if index not in owners:
                blocks.append(jnp.zeros((shard_rows, slot), bf16))
                continue
            which = owners.index(index)
            push = (terms[which] + MUON_BETA * moved[which]).astype(bf16)
            if which == 1:
                none = jnp.zeros_like(push)
                push = jnp.concatenate(
                    [jnp.where(even, push, none), jnp.where(even, none, push)], axis=1
                )
            if push.shape[1] < slot:
                empty = jnp.zeros((shard_rows, slot - push.shape[1]), bf16)
                push = jnp.concatenate([push, empty], axis=1)
            blocks.append(push)
        keep = (0, 2, 3, 4, 5)
        return (
            (jnp.stack(blocks),)
            + tuple(terms)
            + tuple(moved[index] for index in keep)
        )

    def rows_of(width):
        return jax.ShapeDtypeStruct((shard_rows, width), f32)

    widths = (head_width, head_width, head_width, hidden_width, hidden_width, hidden_width)
    made = on_chip(
        advance,
        [jax.ShapeDtypeStruct((data_count, shard_rows, slot), bf16)]
        + [rows_of(width) for width in widths]
        + [rows_of(widths[index]) for index in (0, 2, 3, 4, 5)],
        total_d,
        arrived_gu,
        arrived_attn,
        mom_query,
        mom_key,
        mom_value,
        mom_output,
        mom_gate,
        mom_up,
        mom_down,
        flags=my_tensor.reshape(1),
        limit=24 * 1024 * 1024,
    )
    outgoing, sum_query, part_kv, sum_output, sum_gate, sum_up, sum_down = made[:7]
    moved_query, moved_output, moved_gate, moved_up, moved_down = made[7:]

    owned = exchange(outgoing, DATA).reshape(data_count * shard_rows, slot)

    sum_half = part_kv + swap(part_kv, "tensor", 2)
    sum_other = swap(sum_half, "tensor", 1)
    sum_key = jnp.where(first_core, sum_half, sum_other)
    sum_value = jnp.where(first_core, sum_other, sum_half)
    moved_key = MUON_BETA * mom_key + sum_key
    moved_value = MUON_BETA * mom_value + sum_value
    gain_half = butterfly(gain_term, ("tensor",))
    owned, gain_half, d_input = lax.optimization_barrier((owned, gain_half, d_input))
    across = swap(owned, "tensor", 2)
    grad_gains = butterfly(gain_half, ("minor", "major"))
    across, grad_gains = lax.optimization_barrier((across, grad_gains))
    near = swap(owned, "tensor", 1)
    far = swap(across, "tensor", 1)
    turned = (my_data == owners[1]).astype(jnp.int32).reshape(1)
    ortho = newton_schulz(turned, owned, near, across, far, head_width)
    returned = exchange(ortho.reshape(data_count, shard_rows, slot), DATA)

    weights = (w_query, w_key, w_value, w_output, w_gate, w_up, w_down)
    whole_cols = [
        weights[index].shape[1] * (1 if index in (1, 2) else tensor_count) for index in range(7)
    ]
    places_of = ((0, 0), (1, 0), (1, head_width), (2, 0), (3, 0), (4, 0), (5, 0))

    def renew(back, *held):
        results = []
        for index, weight in enumerate(held):
            which, start = places_of[index]
            update = back[owners[which]][:, start : start + weight.shape[1]].astype(f32)
            factor = 0.2 * math.sqrt(max(model_width, whole_cols[index]))
            results.append(weight - MUON_RATE * (factor * update + MUON_DECAY * weight))
        return tuple(results)

    updated = on_chip(
        renew, [rows_of(weight.shape[1]) for weight in weights], returned, *weights,
        limit=24 * 1024 * 1024,
    )
    next_first = FIRST_DECAY * adam_first + (1.0 - FIRST_DECAY) * grad_gains
    next_second = SECOND_DECAY * adam_second + (1.0 - SECOND_DECAY) * grad_gains * grad_gains
    first_fix = 1.0 - FIRST_DECAY**STEP
    second_fix = 1.0 - SECOND_DECAY**STEP
    new_gains = gains - ADAM_RATE * (next_first / first_fix) / (
        jnp.sqrt(next_second / second_fix) + ADAM_EPSILON
    )
    return (
        block_out,
        d_input,
        sum_query,
        sum_key,
        sum_value,
        sum_output,
        sum_gate,
        sum_up,
        sum_down,
        grad_gains,
        *updated,
        moved_query,
        moved_key,
        moved_value,
        moved_output,
        moved_gate,
        moved_up,
        moved_down,
        new_gains,
        next_first,
        next_second,
    )


def solution(mesh):
    tensor_count = mesh.shape["tensor"]
    split = Mesh(
        mesh.devices.reshape(-1, 2, tensor_count), ("major", "minor", "tensor")
    )
    rows = P(("major", "minor", "tensor"), None)
    both = P(DATA, "tensor")
    data = P(DATA, None)
    matrices = (both, data, data, both, both, both, both)

    return jax.shard_map(
        body,
        mesh=split,
        in_specs=(rows, rows, data) + matrices + matrices + (P(), P(), P()),
        out_specs=(rows, rows) + matrices + (P(),) + matrices + matrices + (P(), P(), P()),
        check_vma=False,
    )
```
